32 devices in a mesh: tok: 8 (over z, x), head: 4 (over y, core).
Axes of the slice: x: 2, y: 2, z: 4, core: 2. Of those that a mesh axis runs over, the one named last changes fastest.
Arguments:
- tokens: bfloat16 [2048, 2048], P(('tok', 'head')), may hold values from -6 to 6
- lengths: int32 [8, 4], P('tok'), may hold values from 1 to 128, 256 in all within a row
- routes: int32 [2048, 8], P('tok'), may hold values from 0 to 15, all different within a row; in each aligned block of 64 rows (0 to 63, 64 to 127, ...) at most 48 rows name the same one
- prefix_kv: bfloat16 [8, 2048, 2, 2048], P('tok', 'head'), may hold values from -6 to 6
- attn_gain: float32 [2048], replicated, may hold values from 0.25 to 1.75
- w_qkv: bfloat16 [2048, 3, 2048], P(None, None, 'head'), may hold values from -0.19605908 to 0.19605908
- w_out: bfloat16 [2048, 2048], P('head'), may hold values from -0.125 to 0.125
- moe_gain: float32 [2048], replicated, may hold values from 0.25 to 1.75
- w_router: bfloat16 [2048, 16], replicated, may hold values from -0.24977002 to 0.24977002
- w_gate: bfloat16 [16, 2048, 1024], P('tok', None, 'head'), may hold values from -0.125 to 0.125
- w_up: bfloat16 [16, 2048, 1024], P('tok', None, 'head'), may hold values from -0.125 to 0.125
- w_down: bfloat16 [16, 1024, 2048], P('tok', 'head'), may hold values from -0.25 to 0.25
Outputs:
- layer_out: bfloat16 [2048, 2048], P(('tok', 'head'))
The draws below stay inside these ranges and needn't reach their ends.
Inputs may be any that keep to these rules, and one draw needn't show every extreme that they name: lengths[i] are the suffix lengths of the 4 requests of the i-th group of 256 tokens, in order; they sum to 256 and the largest in every row is 128. `routes`: each token names 8 different experts; among the 64 tokens of one device (aligned blocks of rows) no expert is named more than 48 times, a bound that some block reaches.
All inputs are finite; a program needn't handle non-finite values.
Results may differ from the reference program's by a relative error of at most 0.007.
Values may be sent and summed in bfloat16 or wider, within the bound.
No kernel may reach another device: no remote copies, remote signals or barrier semaphores. Data moves between devices by JAX's collectives and lax.ppermute only.
A program may use at most 192 MiB of HBM per device.

```python
import math
import jax
import jax.numpy as jnp
import numpy as np
from jax import lax

D = 2048
HEADS = 16
HD = 128
FF = 1024
TOPK = 8
PREFIX = 2048
REQS = 4
REQ_MAX = 128
TOK_DEV = 64
TOK_ROW = 256
TOKENS = 2048
EXPERTS = 16
CAP = 48
N_TOK = 8
N_HEAD = 4


def draw_tokens(key, part):
    value_key = jax.random.fold_in(jax.random.fold_in(key, 11), 0)
    values = jax.random.truncated_normal(value_key, -6.0, 6.0, (TOKENS, D), jnp.float32)
    return values.astype(jnp.bfloat16)


def draw_prefix_kv(key, part):
    value_key = jax.random.fold_in(key, 13)
    layout = (N_TOK, PREFIX, 2, HEADS * HD)
    values = jax.random.truncated_normal(value_key, -6.0, 6.0, layout, jnp.float32)
    return values.astype(jnp.bfloat16)


def draw_w_qkv(key, part):
    value_key = jax.random.fold_in(key, 17)
    layout = (D, 3, HEADS * HD)
    values = jax.random.truncated_normal(value_key, -6.0, 6.0, layout, jnp.float32) * D ** (-0.5)
    return values.astype(jnp.bfloat16)


def draw_w_router(key, part):
    value_key = jax.random.fold_in(key, 19)
    layout = (D, EXPERTS)
    values = jax.random.truncated_normal(value_key, -6.0, 6.0, layout, jnp.float32) * D ** (-0.5)
    return values.astype(jnp.bfloat16)


def block_levels(rng, extent, cuts, least, top_value):
    level = 1.0
    for dim, parts in cuts:
        steps = jax.random.uniform(jax.random.fold_in(jax.random.fold_in(rng, 6), dim), (parts,), jnp.float32, least / len(cuts), top_value / len(cuts))
        level = level * jnp.repeat(jnp.exp(steps), extent[dim] // parts).reshape((-1,) + (1,) * (len(extent) - 1 - dim))
    return level


def length_profile(number_of, total, reach, lean):
    portions = [(1 << 20) // math.isqrt(standing ** lean) + 1 for standing in range(2, number_of + 1)]
    surplus, holding = total - reach - (number_of - 1), [1] * (number_of - 1)
    while surplus > 0:
        candidates = [i for i in range(number_of - 1) if holding[i] < reach]
        mass, remaining = sum([portions[i] for i in candidates]), surplus
        for i in candidates:
            extra = min(reach - holding[i], max(1, remaining * portions[i] // mass), surplus)
            holding[i] = holding[i] + extra
            surplus = surplus - extra
    return np.array([reach] + holding)


def uneven(key, number_of, total, reach, skew):
    if number_of == 2:
        one = jax.random.randint(key, (), max(1, total - reach), min(reach, total - 1) + 1)
        return jnp.stack([one, total - one])
    sizes = jnp.asarray(length_profile(number_of, total, reach, skew), jnp.int32)
    twos = (number_of - 1) // 2
    donor, receiver = sizes[1:1 + 2 * twos:2], sizes[2:2 + 2 * twos:2]
    slack = jnp.minimum(donor - 1, reach - receiver)
    moved = jax.random.randint(jax.random.fold_in(key, 1), (twos,), 0, 1 << 20) % (slack + 1)
    sizes = sizes.at[1:1 + 2 * twos:2].set(donor - moved).at[2:2 + 2 * twos:2].set(receiver + moved)
    return sizes[jax.random.permutation(jax.random.fold_in(key, 2), number_of)]


def assign_block(stream_key, own, number, rows, count, top, most, slope):
    sequence = jax.random.permutation(stream_key, count)
    crowded, ordinary = load_shares(count, rows * top, most, slope, True), load_shares(count, rows * top, most, slope, False)
    places = jnp.arange(count)

    def named(sizes, rotation):
        used = int((sizes > 0).sum())
        fixed = max(1, used // 4)
        shifted = fixed + (places - fixed + rotation * (used - fixed)) % max(1, count - fixed)
        return jnp.zeros((count,), jnp.int32).at[sequence[jnp.where(places < fixed, places, shifted)]].set(jnp.asarray(sizes, jnp.int32))

    sizes = jnp.where(number % 4 == 0, named(crowded, number // 4), named(ordinary, number - number // 4 - 1))
    mixed = jax.random.permutation(jax.random.fold_in(own, 3), count)
    source_of, sink = mixed[0:count // 2 * 2:2], mixed[1:count // 2 * 2:2]
    margin = jnp.minimum(sizes[source_of] - 1, most - sizes[sink]) // 2
    margin = jnp.where((source_of == sequence[0]) | (sink == sequence[0]) | (sizes[sink] == 0), 0, jnp.maximum(margin, 0))
    shifted = jax.random.randint(jax.random.fold_in(own, 4), (count // 2,), 0, 1 << 20) % (margin + 1)
    sizes = sizes.at[source_of].add(-shifted).at[sink].add(shifted)
    items = jnp.searchsorted(jnp.cumsum(sizes), jnp.arange(rows * top), side="right").astype(jnp.int32)
    listing = items.reshape(top, rows).T
    listing = listing[jax.random.permutation(jax.random.fold_in(own, 1), rows)]
    rotation = jax.random.randint(jax.random.fold_in(own, 2), (rows, 1), 0, top)
    return jnp.take_along_axis(listing, (jnp.arange(top)[None, :] + rotation) % top, axis=1)


def load_shares(amount, total, bound, slope, full):
    weights = [(1 << 20) // math.isqrt(rank ** slope) + 1 for rank in range(1, amount + 1)]
    largest = bound if full else min(bound, max(-(-total // amount), total * weights[0] // sum(weights)))
    least = 1 if total - largest >= amount - 1 else 0
    holding, surplus = [largest] + [least] * (amount - 1), total - largest - least * (amount - 1)
    while surplus > 0:
        movable = [i for i in range(1, amount) if holding[i] < largest] or [i for i in range(1, amount) if holding[i] < bound]
        mass, left = sum([weights[i] for i in movable]), surplus
        for i in movable:
            more = min(bound - holding[i], max(1, left * weights[i] // mass), surplus)
            holding[i] = holding[i] + more
            surplus = surplus - more
    return np.array(holding)


def gaussian(rng, dims, scale, limit, cuts=(), kind=jnp.bfloat16):
    entries = scale * jax.random.normal(rng, dims, jnp.float32)
    if cuts:
        entries = entries * block_levels(rng, dims, cuts, -0.22, 0.18)
    return jnp.clip(entries, -limit, limit).astype(kind)


def setup_inputs(seed: int = 0) -> dict:
    arg_keys = jax.random.split(jax.random.key(seed), 13)
    tokens = draw_tokens(jax.random.fold_in(arg_keys[12], 71), 0)
    lengths = jax.vmap(lambda own: uneven(own, REQS, TOK_ROW, REQ_MAX, 2))(jax.random.split(arg_keys[1], N_TOK)).reshape((N_TOK, REQS)).astype(jnp.int32)
    routes_keys = jax.random.split(jax.random.fold_in(arg_keys[2], 1), TOKENS // TOK_DEV)
    routes_turns = jax.random.permutation(jax.random.fold_in(arg_keys[2], 3), TOKENS // TOK_DEV)
    routes = jax.vmap(lambda own, number: assign_block(jax.random.fold_in(arg_keys[2], 2), own, number, TOK_DEV, EXPERTS, TOPK, CAP, 2))(routes_keys, routes_turns).reshape((TOKENS, TOPK))
    prefix_kv = draw_prefix_kv(jax.random.fold_in(arg_keys[12], 71), 0)
    attn_gain = jnp.clip(1.0 + 0.15 * jax.random.normal(arg_keys[4], (D,), jnp.float32), 0.25, 1.75)
    w_qkv = draw_w_qkv(jax.random.fold_in(arg_keys[12], 71), 0)
    w_out = gaussian(arg_keys[6], (HEADS * HD, D), (HEADS * HD) ** -0.5, 0.125, ((0, 4),))
    moe_gain = jnp.clip(1.0 + 0.15 * jax.random.normal(arg_keys[7], (D,), jnp.float32), 0.25, 1.75)
    w_router = draw_w_router(jax.random.fold_in(arg_keys[12], 71), 0)
    w_gate = gaussian(arg_keys[9], (EXPERTS, D, FF), D ** -0.5, 0.125, ((0, 8), (2, 4)))
    w_up = gaussian(arg_keys[10], (EXPERTS, D, FF), D ** -0.5, 0.125, ((0, 8), (2, 4)))
    w_down = gaussian(arg_keys[11], (EXPERTS, FF, D), (FF // 2) ** -0.5, 0.25, ((0, 8), (1, 4)))
    return dict(tokens=tokens, lengths=lengths, routes=routes, prefix_kv=prefix_kv, attn_gain=attn_gain, w_qkv=w_qkv, w_out=w_out, moe_gain=moe_gain, w_router=w_router, w_gate=w_gate, w_up=w_up, w_down=w_down)


rope_base = 10000.0
norm_eps = 1e-06

def rms_scale(values, gain):
    mean_sq = lax.optimization_barrier(jnp.mean(values * values, axis=-1, keepdims=True))
    return (values * lax.rsqrt(mean_sq + norm_eps) * gain).astype(jnp.bfloat16)

def rotate(vectors, position):
    half = vectors.shape[-1] // 2
    freq = rope_base ** (-(jnp.arange(half).astype(jnp.float32) * 2.0) / vectors.shape[-1])
    angle = position[:, None].astype(jnp.float32) * freq[None, :]
    cosine = jnp.cos(angle)[:, None, :]
    sine = jnp.sin(angle)[:, None, :]
    first = vectors[..., :half]
    second = vectors[..., half:]
    return jnp.concatenate([first * cosine - second * sine, second * cosine + first * sine], axis=-1)

def request_layout(lengths_row, rows, prefix):
    ends = jnp.cumsum(lengths_row).astype(jnp.int32)
    index = jnp.arange(rows).astype(jnp.int32)
    passed = (index[:, None] >= ends[None, :]).astype(jnp.int32)
    segment = lax.optimization_barrier(jnp.sum(passed, axis=1))
    offset = index - lax.optimization_barrier(jnp.sum(passed * lengths_row[None, :], axis=1))
    return (segment, prefix + offset)

def attend(query, key_all, value_all, segment, prefix):
    rows = query.shape[0]
    scores = jnp.einsum('qhd,khd->hqk', query.astype(jnp.float32), key_all.astype(jnp.float32))
    scores = scores * query.shape[-1] ** (-0.5)
    allowed = jnp.concatenate([jnp.ones((rows, prefix), bool), segment[:, None] == segment[None, :]], axis=1)
    scores = jnp.where(allowed[None], scores, -1e+30)
    top = lax.optimization_barrier(jnp.max(scores, axis=-1, keepdims=True))
    expo = jnp.exp(scores - top)
    weights = (expo / lax.optimization_barrier(jnp.sum(expo, axis=-1, keepdims=True))).astype(jnp.bfloat16)
    mixed = jnp.einsum('hqk,khd->qhd', weights.astype(jnp.float32), value_all.astype(jnp.float32))
    return mixed.astype(jnp.bfloat16).reshape(rows, -1)

def route_weights(logits, chosen_routes):
    picked = jnp.take_along_axis(logits, chosen_routes, axis=1)
    return jax.nn.softmax(picked, axis=-1)

def ranks_of(blocks, experts):
    onehot = (blocks[..., None] == jnp.arange(experts).astype(jnp.int32)).astype(jnp.int32)
    running = jnp.cumsum(onehot, axis=1)
    return lax.optimization_barrier(jnp.sum(running * onehot, axis=-1)) - 1

def reference(tokens, lengths, routes, prefix_kv, attn_gain, w_qkv, w_out, moe_gain, w_router, w_gate, w_up, w_down):
    rows = TOK_ROW
    width_attn = HEADS * HD
    normed = rms_scale(tokens.astype(jnp.float32), attn_gain)
    flat_qkv = w_qkv.reshape(D, 3 * width_attn)

    def one_row(packed):
        block, lengths_row, cache = packed
        qkv = jnp.dot(block, flat_qkv, preferred_element_type=jnp.float32).reshape(rows, 3, HEADS, HD)
        segment, position = request_layout(lengths_row, rows, PREFIX)
        query = rotate(qkv[:, 0], position).astype(jnp.bfloat16)
        key_new = rotate(qkv[:, 1], position).astype(jnp.bfloat16)
        value_new = qkv[:, 2].astype(jnp.bfloat16)
        key_all = jnp.concatenate([cache[:, 0].reshape(PREFIX, HEADS, HD), key_new], axis=0)
        value_all = jnp.concatenate([cache[:, 1].reshape(PREFIX, HEADS, HD), value_new], axis=0)
        mixed = attend(query, key_all, value_all, segment, PREFIX)
        return jnp.dot(mixed, w_out, preferred_element_type=jnp.float32)
    attn = lax.map(one_row, (normed.reshape(N_TOK, rows, D), lengths, prefix_kv))
    resid = tokens.astype(jnp.float32) + attn.reshape(TOKENS, D)
    normed2 = rms_scale(resid, moe_gain)
    logits = jnp.dot(normed2, w_router, preferred_element_type=jnp.float32)
    weights = route_weights(logits, routes)
    devices = N_TOK * N_HEAD
    rank = ranks_of(routes.reshape(devices, TOK_DEV * TOPK), EXPERTS).reshape(-1)
    flat = routes.reshape(-1)
    count = flat.shape[0]
    device = (jnp.arange(count) // (TOK_DEV * TOPK)).astype(jnp.int32)
    room = devices * CAP
    slot = flat * room + device * CAP + rank
    owner = (jnp.arange(count) // TOPK).astype(jnp.int32)
    table = jnp.full((EXPERTS * room,), TOKENS, jnp.int32).at[slot].set(owner).reshape(EXPERTS, room)
    share = jnp.zeros((EXPERTS * room,), jnp.float32).at[slot].set(weights.reshape(-1)).reshape(EXPERTS, room)
    padded = jnp.concatenate([normed2, jnp.zeros((1, D), jnp.bfloat16)], axis=0)
    quarter = FF // N_HEAD

    def add_expert(total, packed):
        index, gate_w, up_w, down_w, scale = packed
        rows_in = padded[index]
        gate = jnp.dot(rows_in, gate_w, preferred_element_type=jnp.float32)
        up = jnp.dot(rows_in, up_w, preferred_element_type=jnp.float32)
        act = (jax.nn.silu(gate) * up).astype(jnp.bfloat16)
        result = jnp.zeros((room, D), jnp.float32)
        for part in range(N_HEAD):
            piece = jnp.dot(act[:, part * quarter:(part + 1) * quarter], down_w[part * quarter:(part + 1) * quarter], preferred_element_type=jnp.float32)
            piece = lax.optimization_barrier(piece.astype(jnp.bfloat16))
            result = result + piece.astype(jnp.float32)
        return (total.at[index].add(result * scale[:, None]), None)
    total, unused = lax.scan(add_expert, jnp.zeros((TOKENS + 1, D), jnp.float32), (table, w_gate, w_up, w_down, share))
    return (resid + total[:TOKENS]).astype(jnp.bfloat16)
```

```python
import functools

import jax
import jax.numpy as jnp
from jax import lax
from jax.experimental import pallas as pl
from jax.experimental.pallas import tpu as pltpu
from jax.sharding import PartitionSpec as P

HD = 128
PREFIX = 2048
LANES = 128
LOG2E = 1.4426950408889634
rope_base = 10000.0
norm_eps = 1e-06
BF = jnp.bfloat16
F32 = jnp.float32


def params(mib):
    return pltpu.CompilerParams(vmem_limit_bytes=mib << 20)


def cost(flops, moved, exps=0):
    return pl.CostEstimate(flops=flops, bytes_accessed=moved, transcendentals=exps)


def whole(shape):
    return pl.BlockSpec(shape, lambda *_: (0,) * len(shape))


def swap(value, axis, bit):
    size = lax.axis_size(axis)
    return lax.ppermute(value, axis, [(i, i ^ bit) for i in range(size)])


move_x = functools.partial(swap, axis="tok", bit=1)
move_y = functools.partial(swap, axis="head", bit=2)
move_c = functools.partial(swap, axis="head", bit=1)


def from_z(value, k):
    size = lax.axis_size("tok")
    return lax.ppermute(value, "tok", [(i, (i - 2 * k) % size) for i in range(size)])


def to_z(value, k):
    return from_z(value, -k)


def project_kernel(t0, t1, t2, t3, gain, cosine, sine, w, q, k, v, normed):
    part = pl.program_id(0)
    rows = t0.shape[0]

    @pl.when(part == 0)
    def _():
        for i, ref in enumerate((t0, t1, t2, t3)):
            values = ref[...].astype(F32)
            mean_sq = jnp.mean(values * values, axis=-1, keepdims=True)
            scaled = values * lax.rsqrt(mean_sq + norm_eps) * gain[...]
            normed[pl.ds(i * rows, rows), :] = scaled.astype(BF)

    out = jnp.dot(normed[...], w[0], preferred_element_type=F32)

    def rotated(ref):
        for h in range(out.shape[1] // HD):
            one = out[:, h * HD : (h + 1) * HD]
            turned = one * cosine[...] + pltpu.roll(one, HD // 2, 1) * sine[...]
            ref[:, h * HD : (h + 1) * HD] = turned.astype(BF)

    @pl.when(part == 0)
    def _():
        rotated(q)

    @pl.when(part == 1)
    def _():
        rotated(k)

    @pl.when(part == 2)
    def _():
        v[...] = out.astype(BF)


def project(blocks, gain, cosine, sine, w):
    rows, width = blocks[0].shape
    total, local = 4 * rows, w.shape[2]
    shape = jax.ShapeDtypeStruct((total, local), BF)
    return pl.pallas_call(
        project_kernel,
        grid=(3,),
        out_shape=(shape,) * 3,
        in_specs=[whole((rows, width))] * 4
        + [whole((1, width)), whole((total, HD)), whole((total, HD))]
        + [pl.BlockSpec((1, width, local), lambda i: (i, 0, 0))],
        out_specs=(whole((total, local)),) * 3,
        scratch_shapes=[pltpu.VMEM((total, width), BF)],
        compiler_params=params(32),
        cost_estimate=cost(6 * total * width * local, 6 * width * local),
        name="project",
    )(*blocks, gain, cosine, sine, w)


def scores_of(q, keys):
    return lax.dot_general(q, keys, (((1,), (1,)), ((), ())), preferred_element_type=F32)


def attend_pieces(q, pieces):
    scale = HD**-0.5
    scores = []
    for keys, _, allowed in pieces:
        one = scores_of(q, keys)
        scores.append(one if allowed is None else jnp.where(allowed, one, -1e30))
    top = functools.reduce(jnp.maximum, [jnp.max(s, axis=-1, keepdims=True) for s in scores])
    total, mixed = 0.0, 0.0
    for s, (_, values, _) in zip(scores, pieces):
        expo = jnp.exp2((s - top) * (scale * LOG2E))
        total = total + jnp.sum(expo, axis=-1, keepdims=True)
        mixed = mixed + jnp.dot(expo.astype(BF), values, preferred_element_type=F32)
    return mixed / total, top * scale + jnp.log(total)


def own_kernel(group, q, kv_here, kv_there, k, v, seg_row, seg_col, out, stats):
    h = pl.program_id(0)
    same = seg_row[...] == seg_col[...]
    mixed, level = attend_pieces(
        q[...],
        [
            (kv_here[0, :, 0, :], kv_here[0, :, 1, :], None),
            (kv_there[:, 0, :], kv_there[:, 1, :], None),
            (k[...], v[...], same),
        ],
    )
    out[...] = mixed
    lane = lax.broadcasted_iota(jnp.int32, stats.shape, 1)

    @pl.when(h == 0)
    def _():
        stats[...] = jnp.zeros_like(stats)

    stats[...] = jnp.where(lane == h, level, stats[...])


def guest_kernel(group, q, kv_here, kv_there, out):
    h = pl.program_id(0)
    local = out.shape[1] - LANES
    mixed, level = attend_pieces(
        q[...],
        [
            (kv_here[0, :, 0, :], kv_here[0, :, 1, :], None),
            (kv_there[:, 0, :], kv_there[:, 1, :], None),
        ],
    )
    out[:, pl.ds(pl.multiple_of(h * HD, HD), HD)] = mixed.astype(BF)
    lane = lax.broadcasted_iota(jnp.int32, (out.shape[0], LANES), 1)

    @pl.when(h == 0)
    def _():
        out[:, local:] = jnp.zeros((out.shape[0], LANES), BF)

    tail = out[:, local:].astype(F32)
    rest = jnp.broadcast_to(level, tail.shape)
    for i in range(3):
        piece = rest.astype(BF).astype(F32)
        tail = jnp.where(lane == 3 * h + i, piece, tail)
        rest = rest - piece
    out[:, local:] = tail.astype(BF)


def kv_specs(depth, first):
    return [
        pl.BlockSpec((1, depth, 2, HD), lambda i, g: (0, 0, 0, g[0] * 4 + i)),
        pl.BlockSpec((depth, 2, HD), lambda i, g: (0, 0, first + i)),
    ]


def attend_own(group, q, kv, kv_there, k, v, seg_row, seg_col):
    rows, local = q.shape
    heads, depth = local // HD, kv.shape[1]
    block = pl.BlockSpec((rows, HD), lambda i, g: (0, i))
    keys = 2 * depth + rows
    return pl.pallas_call(
        own_kernel,
        grid_spec=pltpu.PrefetchScalarGridSpec(
            num_scalar_prefetch=1,
            grid=(heads,),
            in_specs=[block]
            + kv_specs(depth, 0)
            + [block, block, whole((rows, 1)), whole((1, rows))],
            out_specs=(block, whole((rows, LANES))),
        ),
        out_shape=(
            jax.ShapeDtypeStruct((rows, local), F32),
            jax.ShapeDtypeStruct((rows, LANES), F32),
        ),
        compiler_params=params(32),
        cost_estimate=cost(4 * rows * keys * local, 4 * keys * local, rows * keys * heads),
        name="attend_own",
    )(group, q, kv, kv_there, k, v, seg_row, seg_col)


def attend_guest(group, q, kv, kv_there):
    rows, local = q.shape
    heads, depth = local // HD, kv.shape[1]
    keys = 2 * depth
    return pl.pallas_call(
        guest_kernel,
        grid_spec=pltpu.PrefetchScalarGridSpec(
            num_scalar_prefetch=1,
            grid=(heads,),
            in_specs=[pl.BlockSpec((rows, HD), lambda i, g: (0, i))] + kv_specs(depth, heads),
            out_specs=whole((rows, local + LANES)),
        ),
        out_shape=jax.ShapeDtypeStruct((rows, local + LANES), BF),
        compiler_params=params(32),
        cost_estimate=cost(4 * rows * keys * local, 4 * keys * local, rows * keys * heads),
        name="attend_guest",
    )(group, q, kv, kv_there)


def join_kernel(own, own_stats, guest, w, keep, send):
    local = own.shape[1]
    dev = keep.shape[0] // 2
    heads = []
    for h in range(local // HD):
        cols = slice(h * HD, (h + 1) * HD)
        first = own_stats[:, h : h + 1]
        second = functools.reduce(
            jnp.add, [guest[:, local + 3 * h + i : local + 3 * h + i + 1].astype(F32) for i in range(3)]
        )
        top = jnp.maximum(first, second)
        a, b = jnp.exp(first - top), jnp.exp(second - top)
        heads.append(((own[:, cols] * a + guest[:, cols].astype(F32) * b) / (a + b)).astype(BF))
    mixed = jnp.concatenate(heads, axis=1)
    out = jnp.dot(mixed, w[...], preferred_element_type=F32)
    for i in range(2):
        keep[pl.ds(i * dev, dev), :] = out[2 * i * dev : (2 * i + 1) * dev]
        send[pl.ds(i * dev, dev), :] = out[(2 * i + 1) * dev : (2 * i + 2) * dev].astype(BF)


def join(own, own_stats, guest, w):
    rows, local = own.shape
    width = w.shape[1]
    return pl.pallas_call(
        join_kernel,
        out_shape=(
            jax.ShapeDtypeStruct((rows // 2, width), F32),
            jax.ShapeDtypeStruct((rows // 2, width), BF),
        ),
        compiler_params=params(32),
        cost_estimate=cost(2 * rows * local * width, 2 * local * width + 6 * rows * width // 2),
        name="join",
    )(own, own_stats, guest, w)


def entry_kernel(me, tokens, keep, arrived, gain, w_router, routes, resid, message):
    width = tokens.shape[1]
    experts = w_router.shape[1]
    values = tokens[...].astype(F32) + keep[...] + arrived[...].astype(F32)
    resid[...] = values
    mean_sq = jnp.mean(values * values, axis=-1, keepdims=True)
    normed = (values * lax.rsqrt(mean_sq + norm_eps) * gain[...]).astype(BF)
    message[:, :width] = normed
    logits = jnp.dot(normed, w_router[...], preferred_element_type=F32)
    lane = lax.broadcasted_iota(jnp.int32, logits.shape, 1)
    chosen = lane < 0
    for i in range(routes.shape[1]):
        chosen = chosen | (lane == routes[:, i : i + 1])
    logits = jnp.where(chosen, logits, -jnp.inf)
    expo = jnp.exp(logits - jnp.max(logits, axis=-1, keepdims=True))
    share = expo / jnp.sum(expo, axis=-1, keepdims=True)
    high = share.astype(BF)
    low = (share - high.astype(F32)).astype(BF)
    message[:, width:] = jnp.zeros((tokens.shape[0], LANES), BF)
    message[:, width : width + experts] = high
    message[:, width + LANES // 2 : width + LANES // 2 + experts] = low


def entry(me, tokens, keep, arrived, gain, w_router, routes):
    rows, width = tokens.shape
    experts, topk = w_router.shape[1], routes.shape[1]
    return pl.pallas_call(
        entry_kernel,
        grid_spec=pltpu.PrefetchScalarGridSpec(
            num_scalar_prefetch=1,
            grid=(1,),
            in_specs=[
                whole((rows, width)),
                whole((rows, width)),
                whole((rows, width)),
                whole((1, width)),
                whole((width, experts)),
                pl.BlockSpec((rows, topk), lambda i, m: (m[0], 0)),
            ],
            out_specs=(whole((rows, width)), whole((rows, width + LANES))),
        ),
        out_shape=(
            jax.ShapeDtypeStruct((rows, width), F32),
            jax.ShapeDtypeStruct((rows, width + LANES), BF),
        ),
        compiler_params=params(32),
        cost_estimate=cost(2 * rows * width * LANES, 12 * rows * width),
        name="entry",
    )(me, tokens, keep, arrived, gain, w_router, routes)


def expert_kernel(sizes, tile, group, *refs):
    count = len(sizes)
    pieces, (gate, up, down), out = refs[:count], refs[count : count + 3], refs[count + 3]
    held, sems = refs[count + 4 :]
    width = gate.shape[1]
    step = pl.program_id(0)

    @pl.when(step == 0)
    def _():
        start = 0
        for ref, size in zip(pieces, sizes):
            done = 0
            while done < size:
                take = min(size - done, tile - (start + done) % tile)
                pltpu.make_async_copy(
                    ref.at[pl.ds(done, take)],
                    held.at[pl.ds(start + done, take)],
                    sems.at[(start + done) // tile],
                ).start()
                done += take
            start += size

    here = pl.ds(pl.multiple_of(step * tile, tile), tile)
    pltpu.make_async_copy(held.at[here], held.at[here], sems.at[step]).wait()
    rows = held[here, :width]
    tail = held[here, width:].astype(F32)
    lane = lax.broadcasted_iota(jnp.int32, tail.shape, 1)
    result = None
    for e in range(gate.shape[0]):
        index = group[0] * gate.shape[0] + e
        hit = (lane == index) | (lane == index + LANES // 2)
        share = jnp.sum(jnp.where(hit, tail, 0.0), axis=1, keepdims=True)
        g = jnp.dot(rows, gate[e], preferred_element_type=F32)
        u = jnp.dot(rows, up[e], preferred_element_type=F32)
        act = (g * jax.nn.sigmoid(g) * u * share).astype(BF)
        one = jnp.dot(act, down[e], preferred_element_type=F32)
        result = one if result is None else result + one
    out[...] = result.astype(BF)


def expert_work(group, pieces, gate, up, down, tile=256):
    sizes = [p.shape[0] for p in pieces]
    total = sum(sizes)
    tile = min(tile, total)
    wide, width = pieces[0].shape[1], gate.shape[1]
    flops = 6 * total * gate.shape[0] * width * gate.shape[2]
    return pl.pallas_call(
        functools.partial(expert_kernel, sizes, tile),
        grid_spec=pltpu.PrefetchScalarGridSpec(
            num_scalar_prefetch=1,
            grid=(total // tile,),
            in_specs=[pl.BlockSpec(memory_space=pl.ANY)] * len(pieces)
            + [whole(gate.shape), whole(up.shape), whole(down.shape)],
            out_specs=pl.BlockSpec((tile, width), lambda i, g: (i, 0)),
            scratch_shapes=[
                pltpu.VMEM((total, wide), BF),
                pltpu.SemaphoreType.DMA((total // tile,)),
            ],
        ),
        out_shape=jax.ShapeDtypeStruct((total, width), BF),
        compiler_params=params(48),
        cost_estimate=cost(flops, 4 * total * width + 6 * gate.size),
        name="experts",
    )(group, *pieces, gate, up, down)


def add_bf(*values):
    return functools.reduce(jnp.add, [v.astype(F32) for v in values]).astype(BF)


def gather_level(rows):
    half = rows.shape[1] // 2
    by_y, by_x = move_y(rows), move_x(rows)
    corner_a, corner_b = move_y(by_x[:, :half]), move_x(by_y[:, half:])
    return [rows, by_y, by_x, corner_a, corner_b]


def flat(value):
    return value.reshape(-1, value.shape[-1])


def reduce_level(count, half, kept, sent):
    total = add_bf(kept, move_c(sent))
    width = total.shape[1]
    n = count * 2 * half
    here, by_y, by_x = (total[i * n : (i + 1) * n].reshape(count, 2, half, width) for i in range(3))
    corner_a = total[3 * n : 3 * n + n // 2].reshape(count, half, width)
    corner_b = total[3 * n + n // 2 :].reshape(count, half, width)
    got_a, got_b = move_y(corner_a), move_x(corner_b)
    to_x = jnp.stack([add_bf(by_x[:, 0], got_a), by_x[:, 1]], axis=1)
    to_y = jnp.stack([by_y[:, 0], add_bf(by_y[:, 1], got_b)], axis=1)
    got_x, got_y = move_x(to_x), move_y(to_y)
    return functools.reduce(jnp.add, [v.astype(F32) for v in (here, got_x, got_y)])


def mixture(group, resid, message, gate, up, down):
    rows, width = resid.shape
    depth = lax.axis_size("tok") // 2
    column = [message] + [from_z(message, k) for k in range(1, depth)]
    pieces = gather_level(jnp.stack(column))
    theirs = [flat(move_c(p)) for p in pieces]
    pieces = [flat(p) for p in pieces]
    sent = expert_work(group, theirs, gate, up, down)
    kept = expert_work(group, pieces, gate, up, down)
    sums = reduce_level(depth, rows // 2, kept, sent).reshape(depth, rows, width)
    total = resid + sums[0]
    for k in range(1, depth):
        total = total + to_z(sums[k].astype(BF), k).astype(F32)
    return total.astype(BF)


def request_layout(lengths_row, index):
    ends = jnp.cumsum(lengths_row)
    passed = (index[:, None] >= ends[None, :]).astype(jnp.int32)
    segment = jnp.sum(passed, axis=1)
    offset = index - jnp.sum(passed * lengths_row[None, :], axis=1)
    return segment, PREFIX + offset


def rotation(position):
    half = HD // 2
    freq = rope_base ** (-(jnp.arange(half).astype(F32) * 2.0) / HD)
    angle = position[:, None].astype(F32) * freq[None, :]
    cosine, sine = jnp.cos(angle), jnp.sin(angle)
    return jnp.concatenate([cosine, cosine], 1), jnp.concatenate([-sine, sine], 1)


def on_device(
    tokens, lengths, routes, prefix_kv, attn_gain, w_qkv, w_out, moe_gain, w_router, w_gate, w_up, w_down
):
    dev, width = tokens.shape
    local = w_qkv.shape[2]
    me = lax.axis_index("head")
    group = lax.axis_index("tok").astype(jnp.int32).reshape(1)

    by_c, by_y = move_c(tokens), move_y(tokens)
    blocks = [tokens, by_c, by_y, move_c(by_y)]

    def columns(who):
        return lax.dynamic_slice_in_dim(prefix_kv[0], who * local, local, 2)

    kv_there = move_c(jnp.concatenate([columns(me ^ 1), columns(me ^ 3)], axis=2))

    index = ((me ^ jnp.arange(4))[:, None] * dev + jnp.arange(dev)[None, :]).reshape(-1)
    segment, position = request_layout(lengths[0], index)
    cosine, sine = rotation(position)

    q, k, v = project(
        blocks, attn_gain.reshape(1, -1), cosine, sine, jnp.transpose(w_qkv, (1, 0, 2))
    )
    guest_q = move_y(q)
    mine = me.astype(jnp.int32).reshape(1)
    own, own_stats = attend_own(
        mine, q, prefix_kv, kv_there, k, v, segment.reshape(-1, 1), segment.reshape(1, -1)
    )
    guest = move_y(attend_guest(mine ^ 2, guest_q, prefix_kv, kv_there))
    keep, send = join(own, own_stats, guest, w_out)
    chip = keep + move_c(send).astype(F32)
    arrived = move_y(chip[dev:].astype(BF))
    resid, message = entry(
        mine, tokens, chip[:dev], arrived, moe_gain.reshape(1, -1), w_router, routes
    )
    return mixture(group, resid, message, w_gate, w_up, w_down)


def solution(mesh):
    placed = (
        P(("tok", "head"), None),
        P("tok", None),
        P("tok", None),
        P("tok", "head", None, None),
        P(),
        P(None, None, "head"),
        P("head", None),
        P(),
        P(),
        P("tok", None, "head"),
        P("tok", None, "head"),
        P("tok", "head", None),
    )
    return jax.shard_map(
        on_device, mesh=mesh, in_specs=placed, out_specs=P(("tok", "head"), None), check_vma=False
    )
```

```python
import functools

import jax
import jax.numpy as jnp
from jax import lax
from jax.experimental import pallas as pl
from jax.experimental.pallas import tpu as pltpu
from jax.sharding import PartitionSpec as P

HD = 128
PREFIX = 2048
LANES = 128
LOG2E = 1.4426950408889634
CUTS = 2
rope_base = 10000.0
norm_eps = 1e-06
BF = jnp.bfloat16
F32 = jnp.float32


def params(mib):
    return pltpu.CompilerParams(vmem_limit_bytes=mib << 20)


def cost(flops, moved, exps=0):
    return pl.CostEstimate(flops=flops, bytes_accessed=moved, transcendentals=exps)


def whole(shape):
    return pl.BlockSpec(shape, lambda *_: (0,) * len(shape))


def swap(value, axis, bit):
    size = lax.axis_size(axis)
    return lax.ppermute(value, axis, [(i, i ^ bit) for i in range(size)])


move_x = functools.partial(swap, axis="tok", bit=1)
move_y = functools.partial(swap, axis="head", bit=2)
move_c = functools.partial(swap, axis="head", bit=1)


def from_z(value, k):
    size = lax.axis_size("tok")
    return lax.ppermute(value, "tok", [(i, (i - 2 * k) % size) for i in range(size)])


def to_z(value, k):
    return from_z(value, -k)


def in_hbm(*values):
    return [pltpu.with_memory_space_constraint(v, pltpu.HBM) for v in values]


def project_kernel(t0, t1, t2, t3, gain, cosine, sine, w, q, k, v, normed):
    part = pl.program_id(0)
    rows = t0.shape[0]

    @pl.when(part == 0)
    def _():
        for i, ref in enumerate((t0, t1, t2, t3)):
            values = ref[...].astype(F32)
            mean_sq = jnp.mean(values * values, axis=-1, keepdims=True)
            scaled = values * lax.rsqrt(mean_sq + norm_eps) * gain[...]
            normed[pl.ds(i * rows, rows), :] = scaled.astype(BF)

    out = jnp.dot(normed[...], w[0], preferred_element_type=F32)

    def rotated(ref):
        for h in range(out.shape[1] // HD):
            one = out[:, h * HD : (h + 1) * HD]
            turned = one * cosine[...] + pltpu.roll(one, HD // 2, 1) * sine[...]
            ref[:, h * HD : (h + 1) * HD] = turned.astype(BF)

    @pl.when(part == 0)
    def _():
        rotated(q)

    @pl.when(part == 1)
    def _():
        rotated(k)

    @pl.when(part == 2)
    def _():
        v[...] = out.astype(BF)


def project(blocks, gain, cosine, sine, w):
    rows, width = blocks[0].shape
    total, local = 4 * rows, w.shape[2]
    shape = jax.ShapeDtypeStruct((total, local), BF)
    return pl.pallas_call(
        project_kernel,
        grid=(3,),
        out_shape=(shape,) * 3,
        in_specs=[whole((rows, width))] * 4
        + [whole((1, width)), whole((total, HD)), whole((total, HD))]
        + [pl.BlockSpec((1, width, local), lambda i: (i, 0, 0))],
        out_specs=(whole((total, local)),) * 3,
        scratch_shapes=[pltpu.VMEM((total, width), BF)],
        compiler_params=params(20),
        cost_estimate=cost(6 * total * width * local, 6 * width * local),
        name="project",
    )(*blocks, gain, cosine, sine, w)


def scores_of(q, keys):
    return lax.dot_general(q, keys, (((1,), (1,)), ((), ())), preferred_element_type=F32)


def attend_pieces(q, pieces):
    scale = HD**-0.5
    scores = []
    for keys, _, allowed in pieces:
        one = scores_of(q, keys)
        scores.append(one if allowed is None else jnp.where(allowed, one, -1e30))
    top = functools.reduce(jnp.maximum, [jnp.max(s, axis=-1, keepdims=True) for s in scores])
    total, mixed = 0.0, 0.0
    for s, (_, values, _) in zip(scores, pieces):
        expo = jnp.exp2((s - top) * (scale * LOG2E))
        total = total + jnp.sum(expo, axis=-1, keepdims=True)
        mixed = mixed + jnp.dot(expo.astype(BF), values, preferred_element_type=F32)
    return mixed / total, top * scale + jnp.log(total)


def own_kernel(group, q, kv_here, kv_there, k, v, seg_row, seg_col, out, stats):
    h = pl.program_id(0)
    same = seg_row[...] == seg_col[...]
    mixed, level = attend_pieces(
        q[...],
        [
            (kv_here[0, :, 0, :], kv_here[0, :, 1, :], None),
            (kv_there[:, 0, :], kv_there[:, 1, :], None),
            (k[...], v[...], same),
        ],
    )
    out[...] = mixed
    lane = lax.broadcasted_iota(jnp.int32, stats.shape, 1)

    @pl.when(h == 0)
    def _():
        stats[...] = jnp.zeros_like(stats)

    stats[...] = jnp.where(lane == h, level, stats[...])


def guest_kernel(group, q, kv_here, kv_there, out):
    h = pl.program_id(0)
    local = out.shape[1] - LANES
    mixed, level = attend_pieces(
        q[...],
        [
            (kv_here[0, :, 0, :], kv_here[0, :, 1, :], None),
            (kv_there[:, 0, :], kv_there[:, 1, :], None),
        ],
    )
    out[:, pl.ds(pl.multiple_of(h * HD, HD), HD)] = mixed.astype(BF)
    lane = lax.broadcasted_iota(jnp.int32, (out.shape[0], LANES), 1)

    @pl.when(h == 0)
    def _():
        out[:, local:] = jnp.zeros((out.shape[0], LANES), BF)

    tail = out[:, local:].astype(F32)
    rest = jnp.broadcast_to(level, tail.shape)
    for i in range(3):
        piece = rest.astype(BF).astype(F32)
        tail = jnp.where(lane == 3 * h + i, piece, tail)
        rest = rest - piece
    out[:, local:] = tail.astype(BF)


def kv_specs(depth, heads):
    return [
        pl.BlockSpec((1, depth, 2, HD), lambda i, g: (0, 0, 0, g[0] * heads + i)),
        pl.BlockSpec((depth, 2, HD), lambda i, g: (0, 0, i)),
    ]


def attend_own(group, q, kv, kv_there, k, v, seg_row, seg_col):
    rows, local = q.shape
    heads, depth = local // HD, kv.shape[1]
    block = pl.BlockSpec((rows, HD), lambda i, g: (0, i))
    keys = 2 * depth + rows
    return pl.pallas_call(
        own_kernel,
        grid_spec=pltpu.PrefetchScalarGridSpec(
            num_scalar_prefetch=1,
            grid=(heads,),
            in_specs=[block]
            + kv_specs(depth, heads)
            + [block, block, whole((rows, 1)), whole((1, rows))],
            out_specs=(block, whole((rows, LANES))),
        ),
        out_shape=(
            jax.ShapeDtypeStruct((rows, local), F32),
            jax.ShapeDtypeStruct((rows, LANES), F32),
        ),
        compiler_params=params(20),
        cost_estimate=cost(4 * rows * keys * local, 4 * keys * local, rows * keys * heads),
        name="attend_own",
    )(group, q, kv, kv_there, k, v, seg_row, seg_col)


def attend_guest(group, q, kv, kv_there):
    rows, local = q.shape
    heads, depth = local // HD, kv.shape[1]
    keys = 2 * depth
    return pl.pallas_call(
        guest_kernel,
        grid_spec=pltpu.PrefetchScalarGridSpec(
            num_scalar_prefetch=1,
            grid=(heads,),
            in_specs=[pl.BlockSpec((rows, HD), lambda i, g: (0, i))] + kv_specs(depth, heads),
            out_specs=whole((rows, local + LANES)),
        ),
        out_shape=jax.ShapeDtypeStruct((rows, local + LANES), BF),
        compiler_params=params(20),
        cost_estimate=cost(4 * rows * keys * local, 4 * keys * local, rows * keys * heads),
        name="attend_guest",
    )(group, q, kv, kv_there)


def join_kernel(own, own_stats, guest, w, keep, send):
    local = own.shape[1]
    dev = keep.shape[0] // 2
    heads = []
    for h in range(local // HD):
        cols = slice(h * HD, (h + 1) * HD)
        first = own_stats[:, h : h + 1]
        second = functools.reduce(
            jnp.add, [guest[:, local + 3 * h + i : local + 3 * h + i + 1].astype(F32) for i in range(3)]
        )
        top = jnp.maximum(first, second)
        a, b = jnp.exp(first - top), jnp.exp(second - top)
        heads.append(((own[:, cols] * a + guest[:, cols].astype(F32) * b) / (a + b)).astype(BF))
    mixed = jnp.concatenate(heads, axis=1)
    out = jnp.dot(mixed, w[...], preferred_element_type=F32)
    for i in range(2):
        keep[pl.ds(i * dev, dev), :] = out[2 * i * dev : (2 * i + 1) * dev]
        send[pl.ds(i * dev, dev), :] = out[(2 * i + 1) * dev : (2 * i + 2) * dev].astype(BF)


def join(own, own_stats, guest, w):
    rows, local = own.shape
    width = w.shape[1]
    return pl.pallas_call(
        join_kernel,
        out_shape=(
            jax.ShapeDtypeStruct((rows // 2, width), F32),
            jax.ShapeDtypeStruct((rows // 2, width), BF),
        ),
        compiler_params=params(20),
        cost_estimate=cost(2 * rows * local * width, 2 * local * width + 6 * rows * width // 2),
        name="join",
    )(own, own_stats, guest, w)


def entry_kernel(me, tokens, keep, arrived, gain, w_router, routes, resid, *messages):
    width = tokens.shape[1]
    experts = w_router.shape[1]
    values = tokens[...].astype(F32) + keep[...] + arrived[...].astype(F32)
    resid[...] = values
    mean_sq = jnp.mean(values * values, axis=-1, keepdims=True)
    normed = (values * lax.rsqrt(mean_sq + norm_eps) * gain[...]).astype(BF)
    logits = jnp.dot(normed, w_router[...], preferred_element_type=F32)
    lane = lax.broadcasted_iota(jnp.int32, logits.shape, 1)
    chosen = lane < 0
    for i in range(routes.shape[1]):
        chosen = chosen | (lane == routes[:, i : i + 1])
    logits = jnp.where(chosen, logits, -jnp.inf)
    expo = jnp.exp(logits - jnp.max(logits, axis=-1, keepdims=True))
    share = expo / jnp.sum(expo, axis=-1, keepdims=True)
    high = share.astype(BF)
    low = (share - high.astype(F32)).astype(BF)
    some = tokens.shape[0] // len(messages)
    for i, message in enumerate(messages):
        part = slice(i * some, (i + 1) * some)
        message[:, :width] = normed[part]
        message[:, width:] = jnp.zeros((some, LANES), BF)
        message[:, width : width + experts] = high[part]
        message[:, width + LANES // 2 : width + LANES // 2 + experts] = low[part]


def entry(me, tokens, keep, arrived, gain, w_router, routes, cuts):
    rows, width = tokens.shape
    some = rows // cuts
    experts, topk = w_router.shape[1], routes.shape[1]
    return pl.pallas_call(
        entry_kernel,
        grid_spec=pltpu.PrefetchScalarGridSpec(
            num_scalar_prefetch=1,
            grid=(1,),
            in_specs=[
                whole((rows, width)),
                whole((rows, width)),
                whole((rows, width)),
                whole((1, width)),
                whole((width, experts)),
                pl.BlockSpec((rows, topk), lambda i, m: (m[0], 0)),
            ],
            out_specs=(whole((rows, width)),) + (whole((some, width + LANES)),) * cuts,
        ),
        out_shape=(
            jax.ShapeDtypeStruct((rows, width), F32),
        )
        + (jax.ShapeDtypeStruct((some, width + LANES), BF),) * cuts,
        compiler_params=params(20),
        cost_estimate=cost(2 * rows * width * LANES, 12 * rows * width),
        name="entry",
    )(me, tokens, keep, arrived, gain, w_router, routes)


def expert_kernel(sizes, starts, tile, fetch, group, *refs):
    count = len(sizes)
    pieces, sources, out = refs[:count], refs[count : count + 3], refs[count + 3]
    if fetch:
        *on_chip, held, sems, loads = refs[count + 4 :]
    else:
        on_chip, (held, sems) = sources, refs[count + 4 :]
    gate, up, down = on_chip
    experts, width = gate.shape[0], gate.shape[1]
    step = pl.program_id(0)

    def load(e, i):
        return pltpu.make_async_copy(sources[i].at[e], on_chip[i].at[e], loads.at[e, i])

    def at_first(act):
        if fetch:
            pl.when(step == 0)(act)

    def bring():
        start = 0
        for ref, first, size in zip(pieces, starts, sizes):
            done = 0
            while done < size:
                take = min(size - done, tile - (start + done) % tile)
                pltpu.make_async_copy(
                    ref.at[pl.ds(first + done, take)],
                    held.at[pl.ds(start + done, take)],
                    sems.at[(start + done) // tile],
                ).start()
                done += take
            start += size

    if fetch:

        @pl.when(step == 0)
        def _():
            load(0, 0).start()
            load(0, 1).start()

    pl.when(step == 0)(bring)
    here = pl.ds(pl.multiple_of(step * tile, tile), tile)
    pltpu.make_async_copy(held.at[here], held.at[here], sems.at[step]).wait()
    rows = held[here, :width]
    tail = held[here, width:].astype(F32)
    lane = lax.broadcasted_iota(jnp.int32, tail.shape, 1)
    result = None
    for e in range(experts):
        index = group[0] * experts + e
        hit = (lane == index) | (lane == index + LANES // 2)
        share = jnp.sum(jnp.where(hit, tail, 0.0), axis=1, keepdims=True)

        def before_gate(e=e):
            load(e, 0).wait()
            load(e, 2).start()
            if e + 1 < experts:
                load(e + 1, 0).start()

        def before_up(e=e):
            load(e, 1).wait()
            if e + 1 < experts:
                load(e + 1, 1).start()

        at_first(before_gate)
        g = jnp.dot(rows, gate[e], preferred_element_type=F32)
        at_first(before_up)
        u = jnp.dot(rows, up[e], preferred_element_type=F32)
        act = (g * jax.nn.sigmoid(g) * u * share).astype(BF)
        at_first(lambda e=e: load(e, 2).wait())
        one = jnp.dot(act, down[e], preferred_element_type=F32)
        result = one if result is None else result + one
    out[...] = result.astype(BF)


def expert_call(group, pieces, weights, tile, fetch):
    gate = weights[0]
    sizes = [size for _, _, size in pieces]
    starts = [start for _, start, _ in pieces]
    total = sum(sizes)
    wide, width = pieces[0][0].shape[1], gate.shape[1]
    flops = 6 * total * gate.shape[0] * width * gate.shape[2]
    on_chip = pl.BlockSpec(memory_space=pltpu.VMEM)
    shape = jax.ShapeDtypeStruct((total, width), BF)
    spec = pl.BlockSpec((tile, width), lambda i, g: (i, 0))
    scratch = [pltpu.VMEM((total, wide), BF), pltpu.SemaphoreType.DMA((total // tile,))]
    return pl.pallas_call(
        functools.partial(expert_kernel, sizes, starts, tile, fetch),
        grid_spec=pltpu.PrefetchScalarGridSpec(
            num_scalar_prefetch=1,
            grid=(total // tile,),
            in_specs=[pl.BlockSpec(memory_space=pl.ANY)] * len(pieces)
            + [pl.BlockSpec(memory_space=pltpu.HBM) if fetch else on_chip] * 3,
            out_specs=(spec,) + (on_chip,) * 3 if fetch else spec,
            scratch_shapes=scratch
            + ([pltpu.SemaphoreType.DMA((gate.shape[0], 3))] if fetch else []),
        ),
        out_shape=(shape,) + tuple(jax.ShapeDtypeStruct(w.shape, w.dtype) for w in weights)
        if fetch
        else shape,
        compiler_params=params(20 + (total >> 7)),
        cost_estimate=cost(flops, 4 * total * width + 6 * gate.size),
        name="experts",
    )(group, *[array for array, _, _ in pieces], *weights)


def expert_part(group, pieces, weights, fetch=False, most=512):
    total = sum(size for _, _, size in pieces)
    tile = next(t for t in range(most, 0, -64) if total % t == 0)
    return expert_call(group, pieces, weights, tile, fetch)


def add_bf(*values):
    return functools.reduce(jnp.add, [v.astype(F32) for v in values]).astype(BF)


def after(value, *others):
    return lax.optimization_barrier((value, *others))[0]


def join_rows(*values):
    return jnp.concatenate(values, axis=0)


def sections(total):
    n = total.shape[0] // 4
    return [total[i * n : (i + 1) * n] for i in range(4)]


def reduce_corner(total):
    corner = sections(total)[3]
    half = corner.shape[0] // 2
    return move_y(corner[:half]), move_x(corner[half:])


def reduce_rest(total, got):
    here, by_y, by_x, _ = sections(total)
    half = here.shape[0] // 2
    to_x = join_rows(add_bf(by_x[:half], got[0]), by_x[half:])
    to_y = join_rows(by_y[:half], add_bf(by_y[half:], got[1]))
    got_x, got_y = move_x(to_x), move_y(to_y)
    return functools.reduce(jnp.add, [v.astype(F32) for v in (here, got_x, got_y)])


def mixture(group, resid, messages, weights):
    rows = messages[0].shape[0]
    depth = lax.axis_size("tok") // 2
    n, half = depth * rows, depth * rows // 2
    first, second = messages

    first_z = [from_z(first, k) for k in range(1, depth)]
    second = after(second, *first_z)
    second_z = [from_z(second, k) for k in range(1, depth)]

    here_a = join_rows(first, *first_z)
    here_b = join_rows(second, *second_z)
    y_a, x_a = move_y(here_a), move_x(here_a)
    from_y = move_y(join_rows(x_a[:half], here_b))
    from_x = move_x(join_rows(y_a[half:], here_b))
    corner_y, corner_x = move_y(from_x[half : 2 * half]), move_x(from_y[2 * half :])

    def pieces_of(arrays, skip):
        here, by_y, by_x, by_corner_y, by_corner_x = arrays
        pieces = [(here, 0, n), (by_y, skip, n), (by_x, skip, n)]
        return pieces + [(by_corner_y, 0, half), (by_corner_x, 0, half)]

    there_y, there_x = move_c(from_y), move_c(from_x)
    theirs_a = [move_c(v) for v in (here_a, y_a, x_a)] + [there_y, there_x]
    theirs_b = [move_c(here_b), there_y, there_x, move_c(corner_y), move_c(corner_x)]

    own_a = [here_a, y_a, x_a, from_y, from_x]
    own_b = [here_b, from_y, from_x, corner_y, corner_x]
    kept_a, *held = expert_part(group, pieces_of(own_a, 0), in_hbm(*weights), True)
    theirs_a = after(theirs_a, kept_a, corner_y, corner_x)
    sent_a = expert_part(group, pieces_of(theirs_a, 0), held)
    kept_b = expert_part(group, pieces_of(after(own_b, sent_a), half), held)
    chip_a = add_bf(kept_a, move_c(sent_a))
    got_a = reduce_corner(chip_a)
    sent_b = expert_part(group, pieces_of(after(theirs_b, chip_a, kept_b), half), held)
    sums_a = reduce_rest(chip_a, got_a)
    chip_b = add_bf(kept_b, move_c(sent_b))
    sums_b = reduce_rest(chip_b, reduce_corner(chip_b))

    outs = []
    for i, sums in enumerate((sums_a, sums_b)):
        total = resid[i * rows : (i + 1) * rows] + sums[:rows]
        for k in range(1, depth):
            part = sums[k * rows : (k + 1) * rows].astype(BF)
            total = total + to_z(part, k).astype(F32)
        outs.append(total.astype(BF))
    return jnp.concatenate(outs, axis=0)


def request_layout(lengths_row, index):
    ends = jnp.cumsum(lengths_row)
    passed = (index[:, None] >= ends[None, :]).astype(jnp.int32)
    segment = jnp.sum(passed, axis=1)
    offset = index - jnp.sum(passed * lengths_row[None, :], axis=1)
    return segment, PREFIX + offset


def rotation(position):
    half = HD // 2
    freq = rope_base ** (-(jnp.arange(half).astype(F32) * 2.0) / HD)
    angle = position[:, None].astype(F32) * freq[None, :]
    cosine, sine = jnp.cos(angle), jnp.sin(angle)
    return jnp.concatenate([cosine, cosine], 1), jnp.concatenate([-sine, sine], 1)


def on_device(
    tokens, lengths, routes, prefix_kv, attn_gain, w_qkv, w_out, moe_gain, w_router, w_gate, w_up, w_down
):
    dev, width = tokens.shape
    local = w_qkv.shape[2]
    me = lax.axis_index("head")
    group = lax.axis_index("tok").astype(jnp.int32).reshape(1)

    by_c, by_y = move_c(tokens), move_y(tokens)
    blocks = [tokens, by_c, by_y, move_c(by_y)]

    def columns(who):
        return lax.dynamic_slice_in_dim(prefix_kv[0], who * local, local, 2)

    later = after(me, by_c)
    own_there, guest_there = move_c(columns(later ^ 1)), move_c(columns(later ^ 3))

    index = ((me ^ jnp.arange(4))[:, None] * dev + jnp.arange(dev)[None, :]).reshape(-1)
    segment, position = request_layout(lengths[0], index)
    cosine, sine = rotation(position)

    q, k, v = project(
        blocks, attn_gain.reshape(1, -1), cosine, sine, *in_hbm(jnp.transpose(w_qkv, (1, 0, 2)))
    )
    guest_q = move_y(q)
    mine = me.astype(jnp.int32).reshape(1)
    (cache,) = in_hbm(prefix_kv)
    own, own_stats = attend_own(
        mine, q, cache, own_there, k, v, segment.reshape(-1, 1), segment.reshape(1, -1)
    )
    guest = move_y(attend_guest(mine ^ 2, guest_q, cache, guest_there))
    keep, send = join(own, own_stats, guest, w_out)
    chip = keep + move_c(send).astype(F32)
    arrived = move_y(chip[dev:].astype(BF))
    resid, *messages = entry(
        mine, tokens, chip[:dev], arrived, moe_gain.reshape(1, -1), w_router, routes, CUTS
    )
    return mixture(group, resid, messages, (w_gate, w_up, w_down))


def solution(mesh):
    placed = (
        P(("tok", "head"), None),
        P("tok", None),
        P("tok", None),
        P("tok", "head", None, None),
        P(),
        P(None, None, "head"),
        P("head", None),
        P(),
        P(),
        P("tok", None, "head"),
        P("tok", None, "head"),
        P("tok", "head", None),
    )
    return jax.shard_map(
        on_device, mesh=mesh, in_specs=placed, out_specs=P(("tok", "head"), None), check_vma=False
    )
```

```python
import functools

import jax
import jax.numpy as jnp
from jax import lax
from jax.experimental import pallas as pl
from jax.experimental.pallas import tpu as pltpu
from jax.sharding import PartitionSpec as P

HD = 128
PREFIX = 2048
LANES = 128
LOG2E = 1.4426950408889634
CUTS = 2
OWN_STEPS = 2
rope_base = 10000.0
norm_eps = 1e-06
BF = jnp.bfloat16
F32 = jnp.float32


def params(mib):
    return pltpu.CompilerParams(vmem_limit_bytes=mib << 20)


def cost(flops, moved, exps=0):
    return pl.CostEstimate(flops=flops, bytes_accessed=moved, transcendentals=exps)


def whole(shape):
    return pl.BlockSpec(shape, lambda *_: (0,) * len(shape))


def swap(value, axis, bit):
    size = lax.axis_size(axis)
    return lax.ppermute(value, axis, [(i, i ^ bit) for i in range(size)])


move_x = functools.partial(swap, axis="tok", bit=1)
move_y = functools.partial(swap, axis="head", bit=2)
move_c = functools.partial(swap, axis="head", bit=1)


def from_z(value, k):
    size = lax.axis_size("tok")
    return lax.ppermute(value, "tok", [(i, (i - 2 * k) % size) for i in range(size)])


def to_z(value, k):
    return from_z(value, -k)


def in_hbm(*values):
    return [pltpu.with_memory_space_constraint(v, pltpu.HBM) for v in values]


CHUNKS = 4


def project_kernel(t0, t1, t2, t3, gain, cosine, sine, w_hbm, q, k, v, normed, w, sems):
    rows, width = t0.shape
    depth = width // CHUNKS

    def load(part, i):
        cut = pl.ds(i * depth, depth)
        return pltpu.make_async_copy(w_hbm.at[part, cut], w.at[part, cut], sems.at[part, i])

    for part in range(3):
        for i in range(CHUNKS):
            load(part, i).start()
    for i, ref in enumerate((t0, t1, t2, t3)):
        values = ref[...].astype(F32)
        mean_sq = jnp.mean(values * values, axis=-1, keepdims=True)
        scaled = values * lax.rsqrt(mean_sq + norm_eps) * gain[...]
        normed[pl.ds(i * rows, rows), :] = scaled.astype(BF)
    for part, ref in enumerate((q, k, v)):
        for i in range(CHUNKS):
            load(part, i).wait()
        out = jnp.dot(normed[...], w[part], preferred_element_type=F32)
        if part == 2:
            ref[...] = out.astype(BF)
            continue
        for h in range(out.shape[1] // HD):
            one = out[:, h * HD : (h + 1) * HD]
            turned = one * cosine[...] + pltpu.roll(one, HD // 2, 1) * sine[...]
            ref[:, h * HD : (h + 1) * HD] = turned.astype(BF)


def project(blocks, gain, cosine, sine, w):
    rows, width = blocks[0].shape
    total, local = 4 * rows, w.shape[2]
    shape = jax.ShapeDtypeStruct((total, local), BF)
    return pl.pallas_call(
        project_kernel,
        out_shape=(shape,) * 3,
        in_specs=[pl.BlockSpec(memory_space=pltpu.VMEM)] * 7 + [pl.BlockSpec(memory_space=pltpu.HBM)],
        out_specs=(pl.BlockSpec(memory_space=pltpu.VMEM),) * 3,
        scratch_shapes=[
            pltpu.VMEM((total, width), BF),
            pltpu.VMEM(w.shape, BF),
            pltpu.SemaphoreType.DMA((3, CHUNKS)),
        ],
        compiler_params=params(20),
        cost_estimate=cost(6 * total * width * local, 6 * width * local),
        name="project",
    )(*blocks, gain, cosine, sine, w)


def scores_of(q, keys):
    return lax.dot_general(q, keys, (((1,), (1,)), ((), ())), preferred_element_type=F32)


def attend_pieces(q, pieces):
    scale = HD**-0.5
    scores = []
    for keys, _, allowed in pieces:
        one = scores_of(q, keys)
        scores.append(one if allowed is None else jnp.where(allowed, one, -1e30))
    top = functools.reduce(jnp.maximum, [jnp.max(s, axis=-1, keepdims=True) for s in scores])
    mixed = 0.0
    for s, (_, values, _) in zip(scores, pieces):
        expo = jnp.exp2((s - top) * (scale * LOG2E)).astype(BF)
        wide = jnp.concatenate([values, jnp.ones(values.shape, BF)], axis=1)
        mixed = mixed + jnp.dot(expo, wide, preferred_element_type=F32)
    total = mixed[:, HD:]
    return mixed[:, :HD] / total, top * scale + jnp.log(total[:, :1])


def cached(kv_here, kv_there, cols):
    return [
        (kv_here[0, :, 0, cols], kv_here[0, :, 1, cols], None),
        (kv_there[:, 0, cols], kv_there[:, 1, cols], None),
    ]


def own_kernel(group, q, kv_here, kv_there, k, v, seg_row, seg_col, out, stats):
    step = pl.program_id(0)
    same = seg_row[...] == seg_col[...]
    lane = lax.broadcasted_iota(jnp.int32, stats.shape, 1)
    heads = q.shape[1] // HD

    @pl.when(step == 0)
    def _():
        stats[...] = jnp.zeros_like(stats)

    levels = stats[...]
    for h in range(heads):
        cols = slice(h * HD, (h + 1) * HD)
        pieces = cached(kv_here, kv_there, cols) + [(k[:, cols], v[:, cols], same)]
        mixed, level = attend_pieces(q[:, cols], pieces)
        out[:, cols] = mixed
        levels = jnp.where(lane == step * heads + h, level, levels)
    stats[...] = levels


def guest_kernel(group, q, kv_here, kv_there, out):
    local = out.shape[1] - LANES
    lane = lax.broadcasted_iota(jnp.int32, (out.shape[0], LANES), 1)
    tail = jnp.zeros(lane.shape, F32)
    for h in range(local // HD):
        cols = slice(h * HD, (h + 1) * HD)
        mixed, level = attend_pieces(q[:, cols], cached(kv_here, kv_there, cols))
        out[:, cols] = mixed.astype(BF)
        rest = jnp.broadcast_to(level, tail.shape)
        for i in range(3):
            piece = rest.astype(BF).astype(F32)
            tail = jnp.where(lane == 3 * h + i, piece, tail)
            rest = rest - piece
    out[:, local:] = tail.astype(BF)


def kv_specs(depth, local, steps):
    some = local // steps
    return [
        pl.BlockSpec((1, depth, 2, some), lambda i, g: (0, 0, 0, g[0] * steps + i)),
        pl.BlockSpec((depth, 2, some), lambda i, g: (0, 0, i)),
    ]


def attend_own(group, q, kv, kv_there, k, v, seg_row, seg_col):
    rows, local = q.shape
    heads, depth = local // HD, kv.shape[1]
    steps = OWN_STEPS
    block = pl.BlockSpec((rows, local // steps), lambda i, g: (0, i))
    keys = 2 * depth + rows
    return pl.pallas_call(
        own_kernel,
        grid_spec=pltpu.PrefetchScalarGridSpec(
            num_scalar_prefetch=1,
            grid=(steps,),
            in_specs=[block]
            + kv_specs(depth, local, steps)
            + [block, block, whole((rows, 1)), whole((1, rows))],
            out_specs=(block, whole((rows, LANES))),
        ),
        out_shape=(
            jax.ShapeDtypeStruct((rows, local), F32),
            jax.ShapeDtypeStruct((rows, LANES), F32),
        ),
        compiler_params=params(20),
        cost_estimate=cost(4 * rows * keys * local, 4 * keys * local, rows * keys * heads),
        name="attend_own",
    )(group, q, kv, kv_there, k, v, seg_row, seg_col)


def attend_guest(group, q, kv, kv_there):
    rows, local = q.shape
    heads, depth = local // HD, kv.shape[1]
    keys = 2 * depth
    return pl.pallas_call(
        guest_kernel,
        grid_spec=pltpu.PrefetchScalarGridSpec(
            num_scalar_prefetch=1,
            grid=(1,),
            in_specs=[whole((rows, local))] + kv_specs(depth, local, 1),
            out_specs=whole((rows, local + LANES)),
        ),
        out_shape=jax.ShapeDtypeStruct((rows, local + LANES), BF),
        compiler_params=params(20),
        cost_estimate=cost(4 * rows * keys * local, 4 * keys * local, rows * keys * heads),
        name="attend_guest",
    )(group, q, kv, kv_there)


def join_kernel(own, own_stats, guest, w, keep, send):
    local = own.shape[1]
    dev = keep.shape[0] // 2
    heads = []
    for h in range(local // HD):
        cols = slice(h * HD, (h + 1) * HD)
        first = own_stats[:, h : h + 1]
        second = functools.reduce(
            jnp.add, [guest[:, local + 3 * h + i : local + 3 * h + i + 1].astype(F32) for i in range(3)]
        )
        top = jnp.maximum(first, second)
        a, b = jnp.exp(first - top), jnp.exp(second - top)
        heads.append(((own[:, cols] * a + guest[:, cols].astype(F32) * b) / (a + b)).astype(BF))
    mixed = jnp.concatenate(heads, axis=1)
    out = jnp.dot(mixed, w[...], preferred_element_type=F32)
    for i in range(2):
        keep[pl.ds(i * dev, dev), :] = out[2 * i * dev : (2 * i + 1) * dev]
        send[pl.ds(i * dev, dev), :] = out[(2 * i + 1) * dev : (2 * i + 2) * dev].astype(BF)


def join(own, own_stats, guest, w):
    rows, local = own.shape
    width = w.shape[1]
    return pl.pallas_call(
        join_kernel,
        out_shape=(
            jax.ShapeDtypeStruct((rows // 2, width), F32),
            jax.ShapeDtypeStruct((rows // 2, width), BF),
        ),
        compiler_params=params(20),
        cost_estimate=cost(2 * rows * local * width, 2 * local * width + 6 * rows * width // 2),
        name="join",
    )(own, own_stats, guest, w)


def entry_kernel(me, tokens, keep, arrived, gain, w_router, routes, resid, *messages):
    width = tokens.shape[1]
    experts = w_router.shape[1]
    values = tokens[...].astype(F32) + keep[...] + arrived[...].astype(F32)
    resid[...] = values
    mean_sq = jnp.mean(values * values, axis=-1, keepdims=True)
    normed = (values * lax.rsqrt(mean_sq + norm_eps) * gain[...]).astype(BF)
    logits = jnp.dot(normed, w_router[...], preferred_element_type=F32)
    lane = lax.broadcasted_iota(jnp.int32, logits.shape, 1)
    chosen = lane < 0
    for i in range(routes.shape[1]):
        chosen = chosen | (lane == routes[:, i : i + 1])
    logits = jnp.where(chosen, logits, -jnp.inf)
    expo = jnp.exp(logits - jnp.max(logits, axis=-1, keepdims=True))
    share = expo / jnp.sum(expo, axis=-1, keepdims=True)
    high = share.astype(BF)
    low = (share - high.astype(F32)).astype(BF)
    some = tokens.shape[0] // len(messages)
    for i, message in enumerate(messages):
        part = slice(i * some, (i + 1) * some)
        message[:, :width] = normed[part]
        message[:, width:] = jnp.zeros((some, LANES), BF)
        message[:, width : width + experts] = high[part]
        message[:, width + LANES // 2 : width + LANES // 2 + experts] = low[part]


def entry(me, tokens, keep, arrived, gain, w_router, routes, cuts):
    rows, width = tokens.shape
    some = rows // cuts
    experts, topk = w_router.shape[1], routes.shape[1]
    return pl.pallas_call(
        entry_kernel,
        grid_spec=pltpu.PrefetchScalarGridSpec(
            num_scalar_prefetch=1,
            grid=(1,),
            in_specs=[
                whole((rows, width)),
                whole((rows, width)),
                whole((rows, width)),
                whole((1, width)),
                whole((width, experts)),
                pl.BlockSpec((rows, topk), lambda i, m: (m[0], 0)),
            ],
            out_specs=(whole((rows, width)),) + (whole((some, width + LANES)),) * cuts,
        ),
        out_shape=(
            jax.ShapeDtypeStruct((rows, width), F32),
        )
        + (jax.ShapeDtypeStruct((some, width + LANES), BF),) * cuts,
        compiler_params=params(20),
        cost_estimate=cost(2 * rows * width * LANES, 12 * rows * width),
        name="entry",
    )(me, tokens, keep, arrived, gain, w_router, routes)


def expert_kernel(sizes, tile, group, *refs):
    count = len(sizes)
    pieces, (gate, up, down) = refs[:count], refs[count : count + 3]
    outs, (held, sems) = refs[count + 3 : -2], refs[-2:]
    experts, width = gate.shape[0], gate.shape[1]
    step = pl.program_id(0)

    @pl.when(step == 0)
    def _():
        start = 0
        for ref, size in zip(pieces, sizes):
            done = 0
            while done < size:
                take = min(size - done, tile - (start + done) % tile)
                pltpu.make_async_copy(
                    ref.at[pl.ds(done, take)],
                    held.at[pl.ds(start + done, take)],
                    sems.at[(start + done) // tile],
                ).start()
                done += take
            start += size

    here = pl.ds(pl.multiple_of(step * tile, tile), tile)
    pltpu.make_async_copy(held.at[here], held.at[here], sems.at[step]).wait()
    rows = held[here, :width]
    tail = held[here, width:].astype(F32)
    lane = lax.broadcasted_iota(jnp.int32, tail.shape, 1)
    result = None
    for e in range(experts):
        index = group[0] * experts + e
        hit = (lane == index) | (lane == index + LANES // 2)
        share = jnp.sum(jnp.where(hit, tail, 0.0), axis=1, keepdims=True)
        g = jnp.dot(rows, gate[e], preferred_element_type=F32)
        u = jnp.dot(rows, up[e], preferred_element_type=F32)
        act = (g * jax.nn.sigmoid(g) * u * share).astype(BF)
        one = jnp.dot(act, down[e], preferred_element_type=F32)
        result = one if result is None else result + one
    done = 0
    for out in outs:
        out[...] = result[done : done + out.shape[0]].astype(BF)
        done += out.shape[0]


def expert_part(group, pieces, weights, outs=1, most=512):
    gate = weights[0]
    sizes = [p.shape[0] for p in pieces]
    total = sum(sizes)
    tile = total if outs > 1 else next(t for t in range(most, 0, -64) if total % t == 0)
    wide, width = pieces[0].shape[1], gate.shape[1]
    some = tile // outs
    flops = 6 * total * gate.shape[0] * width * gate.shape[2]
    return pl.pallas_call(
        functools.partial(expert_kernel, sizes, tile),
        grid_spec=pltpu.PrefetchScalarGridSpec(
            num_scalar_prefetch=1,
            grid=(total // tile,),
            in_specs=[pl.BlockSpec(memory_space=pl.ANY)] * len(pieces)
            + [pl.BlockSpec(memory_space=pltpu.VMEM)] * 3,
            out_specs=(pl.BlockSpec((some, width), lambda i, g: (i, 0)),) * outs,
            scratch_shapes=[
                pltpu.VMEM((total, wide), BF),
                pltpu.SemaphoreType.DMA((total // tile,)),
            ],
        ),
        out_shape=(jax.ShapeDtypeStruct((total // outs, width), BF),) * outs,
        compiler_params=params(20 + (total >> 6)),
        cost_estimate=cost(flops, 4 * total * width + 6 * gate.size),
        name="experts",
    )(group, *pieces, *weights)


def add_bf(*values):
    return functools.reduce(jnp.add, [v.astype(F32) for v in values]).astype(BF)


def after(value, *others):
    return lax.optimization_barrier((value, *others))[0]


def join_rows(*values):
    return jnp.concatenate(values, axis=0)


def reduce_corner(kept, sent):
    total = add_bf(kept, move_c(sent))
    half = total.shape[0] // 2
    return move_y(total[:half]), move_x(total[half:])


def reduce_rest(total, got):
    n = total.shape[0] // 3
    half = n // 2
    rows = n // (lax.axis_size("tok") // 2)
    here, by_y, by_x = (total[i * n : (i + 1) * n] for i in range(3))
    to_x = join_rows(add_bf(by_x[:half], got[0]), by_x[half:])
    to_y = join_rows(by_y[:half], add_bf(by_y[half:], got[1]))
    got_x, got_y = move_x(to_x), move_y(to_y)
    total = functools.reduce(jnp.add, [v.astype(F32) for v in (here, got_x, got_y)])
    return total[:rows], total[rows:].astype(BF)


def hold_kernel(count, *refs):
    sources, targets, sems = refs[:count], refs[count : 2 * count], refs[-1]
    copies = []
    for i in range(count):
        some = sources[i].shape[1] // sems.shape[2]
        for e in range(sources[i].shape[0]):
            for j in range(sems.shape[2]):
                rows = pl.ds(j * some, some)
                copies.append(
                    pltpu.make_async_copy(
                        sources[i].at[e, rows], targets[i].at[e, rows], sems.at[i, e, j]
                    )
                )
    for copy in copies:
        copy.start()
    for copy in copies:
        copy.wait()


def hold(*values):
    count = len(values)
    return pl.pallas_call(
        functools.partial(hold_kernel, count),
        out_shape=[jax.ShapeDtypeStruct(v.shape, v.dtype) for v in values],
        in_specs=[pl.BlockSpec(memory_space=pltpu.HBM)] * count,
        out_specs=[pl.BlockSpec(memory_space=pltpu.VMEM)] * count,
        scratch_shapes=[pltpu.SemaphoreType.DMA((count, values[0].shape[0], 2))],
        compiler_params=params(1),
        cost_estimate=cost(0, sum(4 * v.size for v in values)),
        name="hold",
    )(*in_hbm(*values))


def mixture(group, resid, messages, weights):
    rows = messages[0].shape[0]
    depth = lax.axis_size("tok") // 2
    n, half = depth * rows, depth * rows // 2
    first, second = messages

    first_z = [from_z(first, k) for k in range(1, depth)]
    second = after(second, *first_z)
    second_z = [from_z(second, k) for k in range(1, depth)]
    here_a = join_rows(first, *first_z)
    here_b = join_rows(second, *second_z)
    y_a, x_a = move_y(here_a), move_x(here_a)
    held = hold(*after(weights, y_a, x_a))
    corner_a = [move_y(x_a[:half]), move_x(y_a[half:])]
    main_a = [here_a, y_a, x_a]
    their_main_a, their_corner_a = ([move_c(v) for v in values] for values in (main_a, corner_a))
    (sent_a,) = expert_part(group, their_main_a, held)
    leaving_b = after(here_b, *corner_a)
    y_b, x_b = move_y(leaving_b), move_x(leaving_b)
    (kept_a,) = expert_part(group, after(main_a, sent_a), held)
    sent_corner, kept_corner = expert_part(
        group, after(their_corner_a, kept_a) + corner_a, held, 2
    )
    got_a = reduce_corner(after(kept_corner, y_b, x_b), sent_corner)

    corner_b = [move_y(x_b[:half]), move_x(y_b[half:])]
    main_b = [here_b, y_b, x_b]
    their_main_b = [move_c(v) for v in main_b]
    chip_a = add_bf(kept_a, move_c(sent_a))
    (sent_b,) = expert_part(group, after(their_main_b, sent_corner), held)
    (kept_b,) = expert_part(group, after(main_b, sent_b), held)
    corner_b = after(corner_b, kept_b)
    their_corner_b = [move_c(v) for v in corner_b]
    sent_corner, kept_corner = expert_part(group, their_corner_b + corner_b, held, 2)
    got_b = reduce_corner(kept_corner, sent_corner)
    sums_a = reduce_rest(chip_a, got_a)
    chip_b = add_bf(kept_b, move_c(sent_b))
    sums_b = reduce_rest(chip_b, got_b)

    outs, landed = [], []
    for i, (own, rest) in enumerate((sums_a, sums_b)):
        total = resid[i * rows : (i + 1) * rows] + own
        if landed:
            rest = after(rest, *landed)
        parts = [rest[(k - 1) * rows : k * rows] for k in range(1, depth)]
        landed = [to_z(part, k) for k, part in zip(range(1, depth), parts)]
        outs.append(functools.reduce(jnp.add, [v.astype(F32) for v in landed], total).astype(BF))
    return jnp.concatenate(outs, axis=0)


def request_layout(lengths_row, index):
    ends = jnp.cumsum(lengths_row)
    passed = (index[:, None] >= ends[None, :]).astype(jnp.int32)
    segment = jnp.sum(passed, axis=1)
    offset = index - jnp.sum(passed * lengths_row[None, :], axis=1)
    return segment, PREFIX + offset


def rotation(position):
    half = HD // 2
    freq = rope_base ** (-(jnp.arange(half).astype(F32) * 2.0) / HD)
    angle = position[:, None].astype(F32) * freq[None, :]
    cosine, sine = jnp.cos(angle), jnp.sin(angle)
    return jnp.concatenate([cosine, cosine], 1), jnp.concatenate([-sine, sine], 1)


def on_device(
    tokens, lengths, routes, prefix_kv, attn_gain, w_qkv, w_out, moe_gain, w_router, w_gate, w_up, w_down
):
    dev, width = tokens.shape
    local = w_qkv.shape[2]
    me = lax.axis_index("head")
    group = lax.axis_index("tok").astype(jnp.int32).reshape(1)

    by_c, by_y = move_c(tokens), move_y(tokens)
    blocks = [tokens, by_c, by_y, move_c(by_y)]

    def columns(who):
        return lax.dynamic_slice_in_dim(prefix_kv[0], who * local, local, 2)

    later = after(me, by_c)
    own_there, guest_there = move_c(columns(later ^ 1)), move_c(columns(later ^ 3))

    index = ((me ^ jnp.arange(4))[:, None] * dev + jnp.arange(dev)[None, :]).reshape(-1)
    segment, position = request_layout(lengths[0], index)
    cosine, sine = rotation(position)

    q, k, v = project(
        blocks, attn_gain.reshape(1, -1), cosine, sine, *in_hbm(jnp.transpose(w_qkv, (1, 0, 2)))
    )
    guest_q = move_y(q)
    mine = me.astype(jnp.int32).reshape(1)
    (cache,) = in_hbm(prefix_kv)
    own, own_stats = attend_own(
        mine, q, cache, own_there, k, v, segment.reshape(-1, 1), segment.reshape(1, -1)
    )
    guest = move_y(attend_guest(mine ^ 2, guest_q, cache, guest_there))
    keep, send = join(own, own_stats, guest, w_out)
    chip = keep + move_c(send).astype(F32)
    arrived = move_y(chip[dev:].astype(BF))
    resid, *messages = entry(
        mine, tokens, chip[:dev], arrived, moe_gain.reshape(1, -1), w_router, routes, CUTS
    )
    return mixture(group, resid, messages, (w_gate, w_up, w_down))


def solution(mesh):
    placed = (
        P(("tok", "head"), None),
        P("tok", None),
        P("tok", None),
        P("tok", "head", None, None),
        P(),
        P(None, None, "head"),
        P("head", None),
        P(),
        P(),
        P("tok", None, "head"),
        P("tok", None, "head"),
        P("tok", "head", None),
    )
    return jax.shard_map(
        on_device, mesh=mesh, in_specs=placed, out_specs=P(("tok", "head"), None), check_vma=False
    )
```

```python
import functools

import jax
import jax.numpy as jnp
from jax import lax
from jax.experimental import pallas as pl
from jax.experimental.pallas import tpu as pltpu
from jax.sharding import PartitionSpec as P

HD = 128
PREFIX = 2048
LANES = 128
LOG2E = 1.4426950408889634
CUTS = 2
PARTS = 2
rope_base = 10000.0
norm_eps = 1e-06
BF = jnp.bfloat16
F32 = jnp.float32


def params(mib):
    return pltpu.CompilerParams(vmem_limit_bytes=mib << 20)


def cost(flops, moved, exps=0):
    return pl.CostEstimate(flops=flops, bytes_accessed=moved, transcendentals=exps)


def whole(shape):
    return pl.BlockSpec(shape, lambda *_: (0,) * len(shape))


def swap(value, axis, bit):
    size = lax.axis_size(axis)
    return lax.ppermute(value, axis, [(i, i ^ bit) for i in range(size)])


move_x = functools.partial(swap, axis="tok", bit=1)
move_y = functools.partial(swap, axis="head", bit=2)
move_c = functools.partial(swap, axis="head", bit=1)


def from_z(value, k):
    size = lax.axis_size("tok")
    return lax.ppermute(value, "tok", [(i, (i - 2 * k) % size) for i in range(size)])


def to_z(value, k):
    return from_z(value, -k)


def in_hbm(*values):
    return [pltpu.with_memory_space_constraint(v, pltpu.HBM) for v in values]


def stage_kernel(who, kv, own, guest, sems):
    local = own.shape[2]
    some = kv.shape[1] // sems.shape[1]
    copies = []
    for i, (bit, target) in enumerate(((1, own), (3, guest))):
        cols = pl.ds(pl.multiple_of((who[0] ^ bit) * local, local), local)
        for j in range(sems.shape[1]):
            rows = pl.ds(j * some, some)
            copies.append(
                pltpu.make_async_copy(kv.at[0, rows, :, cols], target.at[rows], sems.at[i, j])
            )
    for copy in copies:
        copy.start()
    for copy in copies:
        copy.wait()


def stage(who, kv, local):
    depth = kv.shape[1]
    piece = jax.ShapeDtypeStruct((depth, 2, local), BF)
    return pl.pallas_call(
        stage_kernel,
        grid_spec=pltpu.PrefetchScalarGridSpec(
            num_scalar_prefetch=1,
            grid=(1,),
            in_specs=[pl.BlockSpec(memory_space=pltpu.HBM)],
            out_specs=[whole(piece.shape)] * 2,
            scratch_shapes=[pltpu.SemaphoreType.DMA((2, 4))],
        ),
        out_shape=[piece, piece],
        compiler_params=params(8),
        cost_estimate=cost(0, 8 * piece.size),
        name="stage",
    )(who, *in_hbm(kv))


def project_kernel(t0, t1, t2, t3, gain, cosine, sine, w, *refs):
    *queries, k, v, normed = refs
    rows = t0.shape[0]
    for i, ref in enumerate((t0, t1, t2, t3)):
        values = ref[...].astype(F32)
        mean_sq = jnp.mean(values * values, axis=-1, keepdims=True)
        scaled = values * lax.rsqrt(mean_sq + norm_eps) * gain[...]
        normed[pl.ds(i * rows, rows), :] = scaled.astype(BF)
    for part, outs in enumerate((queries, [k], [v])):
        out = jnp.dot(normed[...], w[part], preferred_element_type=F32)
        if part == 2:
            v[...] = out.astype(BF)
            continue
        heads = out.shape[1] // HD
        for h in range(heads):
            one = out[:, h * HD : (h + 1) * HD]
            turned = one * cosine[...] + pltpu.roll(one, HD // 2, 1) * sine[...]
            some = heads // len(outs)
            outs[h // some][:, h % some * HD : (h % some + 1) * HD] = turned.astype(BF)


def project(blocks, gain, cosine, sine, w):
    rows, width = blocks[0].shape
    total, local = 4 * rows, w.shape[2]
    widths = [local // PARTS] * PARTS + [local, local]
    return pl.pallas_call(
        project_kernel,
        out_shape=[jax.ShapeDtypeStruct((total, one), BF) for one in widths],
        in_specs=[pl.BlockSpec(memory_space=pltpu.VMEM)] * 8,
        out_specs=[pl.BlockSpec(memory_space=pltpu.VMEM)] * len(widths),
        scratch_shapes=[pltpu.VMEM((total, width), BF)],
        compiler_params=params(20),
        cost_estimate=cost(6 * total * width * local, 6 * width * local),
        name="project",
    )(*blocks, gain, cosine, sine, w)


def scores_of(q, keys):
    return lax.dot_general(q, keys, (((1,), (1,)), ((), ())), preferred_element_type=F32)


def attend_pieces(q, pieces):
    scale = HD**-0.5
    scores = []
    for keys, _, allowed in pieces:
        one = scores_of(q, keys)
        scores.append(one if allowed is None else jnp.where(allowed, one, -1e30))
    top = functools.reduce(jnp.maximum, [jnp.max(s, axis=-1, keepdims=True) for s in scores])
    mixed = 0.0
    for s, (_, values, _) in zip(scores, pieces):
        expo = jnp.exp2((s - top) * (scale * LOG2E)).astype(BF)
        wide = jnp.concatenate([values, jnp.ones(values.shape, BF)], axis=1)
        mixed = mixed + jnp.dot(expo, wide, preferred_element_type=F32)
    total = mixed[:, HD:]
    return mixed[:, :HD] / total, top * scale + jnp.log(total[:, :1])


def cached(kv_here, kv_there, cols):
    return [
        (kv_here[0, :, 0, cols], kv_here[0, :, 1, cols], None),
        (kv_there[:, 0, cols], kv_there[:, 1, cols], None),
    ]


def own_kernel(group, q, kv_here, kv_there, k, v, seg_row, seg_col, out, stats):
    same = seg_row[...] == seg_col[...]
    lane = lax.broadcasted_iota(jnp.int32, stats.shape, 1)
    levels = jnp.zeros(stats.shape, F32)
    for h in range(q.shape[1] // HD):
        cols = slice(h * HD, (h + 1) * HD)
        pieces = cached(kv_here, kv_there, cols) + [(k[:, cols], v[:, cols], same)]
        mixed, level = attend_pieces(q[:, cols], pieces)
        out[:, cols] = mixed
        levels = jnp.where(lane == h, level, levels)
    stats[...] = levels


def guest_kernel(group, q, kv_here, kv_there, out):
    local = out.shape[1] - LANES
    lane = lax.broadcasted_iota(jnp.int32, (out.shape[0], LANES), 1)
    tail = jnp.zeros(lane.shape, F32)
    for h in range(local // HD):
        cols = slice(h * HD, (h + 1) * HD)
        mixed, level = attend_pieces(q[:, cols], cached(kv_here, kv_there, cols))
        out[:, cols] = mixed.astype(BF)
        rest = jnp.broadcast_to(level, tail.shape)
        for i in range(3):
            piece = rest.astype(BF).astype(F32)
            tail = jnp.where(lane == 3 * h + i, piece, tail)
            rest = rest - piece
    out[:, local:] = tail.astype(BF)


def kv_specs(depth, some, part):
    return [
        pl.BlockSpec((1, depth, 2, some), lambda i, g: (0, 0, 0, g[0] * PARTS + part)),
        pl.BlockSpec((depth, 2, some), lambda i, g: (0, 0, part)),
    ]


def attend_own(group, part, q, kv, kv_there, k, v, seg_row, seg_col):
    rows, some = q.shape
    depth = kv.shape[1]
    block = pl.BlockSpec((rows, some), lambda i, g: (0, part))
    keys = 2 * depth + rows
    return pl.pallas_call(
        own_kernel,
        grid_spec=pltpu.PrefetchScalarGridSpec(
            num_scalar_prefetch=1,
            grid=(1,),
            in_specs=[whole((rows, some))]
            + kv_specs(depth, some, part)
            + [block, block, whole((rows, 1)), whole((1, rows))],
            out_specs=(whole((rows, some)), whole((rows, LANES))),
        ),
        out_shape=(
            jax.ShapeDtypeStruct((rows, some), F32),
            jax.ShapeDtypeStruct((rows, LANES), F32),
        ),
        compiler_params=params(20),
        cost_estimate=cost(4 * rows * keys * some, 4 * keys * some, rows * keys * some // HD),
        name="attend_own",
    )(group, q, kv, kv_there, k, v, seg_row, seg_col)


def attend_guest(group, part, q, kv, kv_there):
    rows, some = q.shape
    depth = kv.shape[1]
    keys = 2 * depth
    return pl.pallas_call(
        guest_kernel,
        grid_spec=pltpu.PrefetchScalarGridSpec(
            num_scalar_prefetch=1,
            grid=(1,),
            in_specs=[whole((rows, some))] + kv_specs(depth, some, part),
            out_specs=whole((rows, some + LANES)),
        ),
        out_shape=jax.ShapeDtypeStruct((rows, some + LANES), BF),
        compiler_params=params(20),
        cost_estimate=cost(4 * rows * keys * some, 4 * keys * some, rows * keys * some // HD),
        name="attend_guest",
    )(group, q, kv, kv_there)


def join_kernel(*refs):
    owns, levels, guests = (refs[i * PARTS : (i + 1) * PARTS] for i in range(3))
    w, keep, send = refs[3 * PARTS :]
    dev = keep.shape[0] // 2
    heads = []
    for own, stats, guest in zip(owns, levels, guests):
        some = own.shape[1]
        for h in range(some // HD):
            cols = slice(h * HD, (h + 1) * HD)
            first = stats[:, h : h + 1]
            start = some + 3 * h
            thirds = [guest[:, start + i : start + i + 1].astype(F32) for i in range(3)]
            second = functools.reduce(jnp.add, thirds)
            top = jnp.maximum(first, second)
            a, b = jnp.exp(first - top), jnp.exp(second - top)
            both = own[:, cols] * a + guest[:, cols].astype(F32) * b
            heads.append((both / (a + b)).astype(BF))
    mixed = jnp.concatenate(heads, axis=1)
    out = jnp.dot(mixed, w[...], preferred_element_type=F32)
    for i in range(2):
        keep[pl.ds(i * dev, dev), :] = out[2 * i * dev : (2 * i + 1) * dev]
        send[pl.ds(i * dev, dev), :] = out[(2 * i + 1) * dev : (2 * i + 2) * dev].astype(BF)


def join(owns, levels, guests, w):
    rows = owns[0].shape[0]
    local, width = w.shape
    return pl.pallas_call(
        join_kernel,
        out_shape=(
            jax.ShapeDtypeStruct((rows // 2, width), F32),
            jax.ShapeDtypeStruct((rows // 2, width), BF),
        ),
        compiler_params=params(20),
        cost_estimate=cost(2 * rows * local * width, 2 * local * width + 6 * rows * width // 2),
        name="join",
    )(*owns, *levels, *guests, w)


def entry_kernel(me, tokens, keep, arrived, gain, w_router, routes, resid, *messages):
    width = tokens.shape[1]
    experts = w_router.shape[1]
    values = tokens[...].astype(F32) + keep[...] + arrived[...].astype(F32)
    resid[...] = values
    mean_sq = jnp.mean(values * values, axis=-1, keepdims=True)
    normed = (values * lax.rsqrt(mean_sq + norm_eps) * gain[...]).astype(BF)
    logits = jnp.dot(normed, w_router[...], preferred_element_type=F32)
    lane = lax.broadcasted_iota(jnp.int32, logits.shape, 1)
    chosen = lane < 0
    for i in range(routes.shape[1]):
        chosen = chosen | (lane == routes[:, i : i + 1])
    logits = jnp.where(chosen, logits, -jnp.inf)
    expo = jnp.exp(logits - jnp.max(logits, axis=-1, keepdims=True))
    share = expo / jnp.sum(expo, axis=-1, keepdims=True)
    high = share.astype(BF)
    low = (share - high.astype(F32)).astype(BF)
    some = tokens.shape[0] // len(messages)
    for i, message in enumerate(messages):
        part = slice(i * some, (i + 1) * some)
        message[:, :width] = normed[part]
        message[:, width:] = jnp.zeros((some, LANES), BF)
        message[:, width : width + experts] = high[part]
        message[:, width + LANES // 2 : width + LANES // 2 + experts] = low[part]


def entry(me, tokens, keep, arrived, gain, w_router, routes, cuts):
    rows, width = tokens.shape
    some = rows // cuts
    experts, topk = w_router.shape[1], routes.shape[1]
    return pl.pallas_call(
        entry_kernel,
        grid_spec=pltpu.PrefetchScalarGridSpec(
            num_scalar_prefetch=1,
            grid=(1,),
            in_specs=[
                whole((rows, width)),
                whole((rows, width)),
                whole((rows, width)),
                whole((1, width)),
                whole((width, experts)),
                pl.BlockSpec((rows, topk), lambda i, m: (m[0], 0)),
            ],
            out_specs=(whole((rows, width)),) + (whole((some, width + LANES)),) * cuts,
        ),
        out_shape=(
            jax.ShapeDtypeStruct((rows, width), F32),
        )
        + (jax.ShapeDtypeStruct((some, width + LANES), BF),) * cuts,
        compiler_params=params(20),
        cost_estimate=cost(2 * rows * width * LANES, 12 * rows * width),
        name="entry",
    )(me, tokens, keep, arrived, gain, w_router, routes)


def expert_kernel(sizes, tile, group, *refs):
    count = len(sizes)
    pieces, (gate, up, down) = refs[:count], refs[count : count + 3]
    outs, (held, sems) = refs[count + 3 : -2], refs[-2:]
    experts, width = gate.shape[0], gate.shape[1]
    step = pl.program_id(0)

    @pl.when(step == 0)
    def _():
        start = 0
        for ref, size in zip(pieces, sizes):
            done = 0
            while done < size:
                take = min(size - done, tile - (start + done) % tile)
                pltpu.make_async_copy(
                    ref.at[pl.ds(done, take)],
                    held.at[pl.ds(start + done, take)],
                    sems.at[(start + done) // tile],
                ).start()
                done += take
            start += size

    here = pl.ds(pl.multiple_of(step * tile, tile), tile)
    pltpu.make_async_copy(held.at[here], held.at[here], sems.at[step]).wait()
    rows = held[here, :width]
    tail = held[here, width:].astype(F32)
    lane = lax.broadcasted_iota(jnp.int32, tail.shape, 1)
    result = None
    for e in range(experts):
        index = group[0] * experts + e
        hit = (lane == index) | (lane == index + LANES // 2)
        share = jnp.sum(jnp.where(hit, tail, 0.0), axis=1, keepdims=True)
        g = jnp.dot(rows, gate[e], preferred_element_type=F32)
        u = jnp.dot(rows, up[e], preferred_element_type=F32)
        act = (g * jax.nn.sigmoid(g) * u * share).astype(BF)
        one = jnp.dot(act, down[e], preferred_element_type=F32)
        result = one if result is None else result + one
    done = 0
    for out in outs:
        out[...] = result[done : done + out.shape[0]].astype(BF)
        done += out.shape[0]


def expert_part(group, pieces, weights, outs=1, most=512):
    gate = weights[0]
    sizes = [p.shape[0] for p in pieces]
    total = sum(sizes)
    tile = total if outs > 1 else next(t for t in range(most, 0, -64) if total % t == 0)
    wide, width = pieces[0].shape[1], gate.shape[1]
    some = tile // outs
    flops = 6 * total * gate.shape[0] * width * gate.shape[2]
    return pl.pallas_call(
        functools.partial(expert_kernel, sizes, tile),
        grid_spec=pltpu.PrefetchScalarGridSpec(
            num_scalar_prefetch=1,
            grid=(total // tile,),
            in_specs=[pl.BlockSpec(memory_space=pl.ANY)] * len(pieces)
            + [pl.BlockSpec(memory_space=pltpu.VMEM)] * 3,
            out_specs=(pl.BlockSpec((some, width), lambda i, g: (i, 0)),) * outs,
            scratch_shapes=[
                pltpu.VMEM((total, wide), BF),
                pltpu.SemaphoreType.DMA((total // tile,)),
            ],
        ),
        out_shape=(jax.ShapeDtypeStruct((total // outs, width), BF),) * outs,
        compiler_params=params(20 + (total >> 6)),
        cost_estimate=cost(flops, 4 * total * width + 6 * gate.size),
        name="experts",
    )(group, *pieces, *weights)


def add_bf(*values):
    return functools.reduce(jnp.add, [v.astype(F32) for v in values]).astype(BF)


def after(value, *others):
    return lax.optimization_barrier((value, *others))[0]


def join_rows(*values):
    return jnp.concatenate(values, axis=0)


def reduce_corner(kept, sent):
    total = add_bf(kept, move_c(sent))
    half = total.shape[0] // 2
    return move_y(total[:half]), move_x(total[half:])


def reduce_rest(total, got):
    n = total.shape[0] // 3
    half = n // 2
    rows = n // (lax.axis_size("tok") // 2)
    here, by_y, by_x = (total[i * n : (i + 1) * n] for i in range(3))
    to_x = join_rows(add_bf(by_x[:half], got[0]), by_x[half:])
    to_y = join_rows(by_y[:half], add_bf(by_y[half:], got[1]))
    got_x, got_y = move_x(to_x), move_y(to_y)
    total = functools.reduce(jnp.add, [v.astype(F32) for v in (here, got_x, got_y)])
    return total[:rows], total[rows:].astype(BF)


def hold_kernel(count, *refs):
    sources, targets, sems = refs[:count], refs[count : 2 * count], refs[-1]
    copies = []
    for i in range(count):
        some = sources[i].shape[1] // sems.shape[2]
        for e in range(sources[i].shape[0]):
            for j in range(sems.shape[2]):
                rows = pl.ds(j * some, some)
                copies.append(
                    pltpu.make_async_copy(
                        sources[i].at[e, rows], targets[i].at[e, rows], sems.at[i, e, j]
                    )
                )
    for copy in copies:
        copy.start()
    for copy in copies:
        copy.wait()


def hold(*values):
    count = len(values)
    return pl.pallas_call(
        functools.partial(hold_kernel, count),
        out_shape=[jax.ShapeDtypeStruct(v.shape, v.dtype) for v in values],
        in_specs=[pl.BlockSpec(memory_space=pltpu.HBM)] * count,
        out_specs=[pl.BlockSpec(memory_space=pltpu.VMEM)] * count,
        scratch_shapes=[pltpu.SemaphoreType.DMA((count, values[0].shape[0], 2))],
        compiler_params=params(1),
        cost_estimate=cost(0, sum(4 * v.size for v in values)),
        name="hold",
    )(*in_hbm(*values))


def mixture(group, resid, messages, weights):
    rows = messages[0].shape[0]
    depth = lax.axis_size("tok") // 2
    n, half = depth * rows, depth * rows // 2
    first, second = messages

    first_z = [from_z(first, k) for k in range(1, depth)]
    second = after(second, *first_z)
    second_z = [from_z(second, k) for k in range(1, depth)]
    here_a = join_rows(first, *first_z)
    y_a, x_a = move_y(here_a), move_x(here_a)
    held = hold(*after(weights, y_a, x_a))
    corner_a = [move_y(x_a[:half]), move_x(y_a[half:])]
    main_a = [here_a, y_a, x_a]
    their_main_a, their_corner_a = ([move_c(v) for v in values] for values in (main_a, corner_a))
    (sent_a,) = expert_part(group, their_main_a, held)
    here_b = join_rows(second, *after(second_z, *corner_a))
    leaving_b = here_b
    y_b, x_b = move_y(leaving_b), move_x(leaving_b)
    (kept_a,) = expert_part(group, after(main_a, sent_a), held)
    sent_corner, kept_corner = expert_part(
        group, after(their_corner_a, kept_a) + corner_a, held, 2
    )
    got_a = reduce_corner(after(kept_corner, y_b, x_b), sent_corner)

    corner_b = [move_y(x_b[:half]), move_x(y_b[half:])]
    main_b = [here_b, y_b, x_b]
    their_main_b = [move_c(v) for v in main_b]
    chip_a = add_bf(kept_a, move_c(sent_a))
    (sent_b,) = expert_part(group, after(their_main_b, sent_corner), held)
    (kept_b,) = expert_part(group, after(main_b, sent_b), held)
    corner_b = after(corner_b, kept_b)
    their_corner_b = [move_c(v) for v in corner_b]
    sent_corner, kept_corner = expert_part(group, their_corner_b + corner_b, held, 2)
    got_b = reduce_corner(kept_corner, sent_corner)
    sums_a = reduce_rest(chip_a, got_a)
    chip_b = add_bf(kept_b, move_c(sent_b))
    sums_b = reduce_rest(chip_b, got_b)

    outs, landed = [], []
    for i, (own, rest) in enumerate((sums_a, sums_b)):
        total = resid[i * rows : (i + 1) * rows] + own
        if landed:
            rest = after(rest, *landed)
        parts = [rest[(k - 1) * rows : k * rows] for k in range(1, depth)]
        landed = [to_z(part, k) for k, part in zip(range(1, depth), parts)]
        outs.append(functools.reduce(jnp.add, [v.astype(F32) for v in landed], total).astype(BF))
    return jnp.concatenate(outs, axis=0)


def request_layout(lengths_row, index):
    ends = jnp.cumsum(lengths_row)
    passed = (index[:, None] >= ends[None, :]).astype(jnp.int32)
    segment = jnp.sum(passed, axis=1)
    offset = index - jnp.sum(passed * lengths_row[None, :], axis=1)
    return segment, PREFIX + offset


def rotation(position):
    half = HD // 2
    freq = rope_base ** (-(jnp.arange(half).astype(F32) * 2.0) / HD)
    angle = position[:, None].astype(F32) * freq[None, :]
    cosine, sine = jnp.cos(angle), jnp.sin(angle)
    return jnp.concatenate([cosine, cosine], 1), jnp.concatenate([-sine, sine], 1)


def on_device(
    tokens, lengths, routes, prefix_kv, attn_gain, w_qkv, w_out, moe_gain, w_router, w_gate, w_up, w_down
):
    dev, width = tokens.shape
    local = w_qkv.shape[2]
    me = lax.axis_index("head")
    group = lax.axis_index("tok").astype(jnp.int32).reshape(1)

    by_c, by_y = move_c(tokens), move_y(tokens)
    mine = me.astype(jnp.int32).reshape(1)
    own_there, guest_there = stage(mine, prefix_kv, local)
    (w_held,) = hold(jnp.transpose(w_qkv, (1, 0, 2)))
    blocks = [tokens, by_c, by_y, move_c(after(by_y, w_held, guest_there))]

    own_there, guest_there = move_c(own_there), move_c(guest_there)

    index = ((me ^ jnp.arange(4))[:, None] * dev + jnp.arange(dev)[None, :]).reshape(-1)
    segment, position = request_layout(lengths[0], index)
    cosine, sine = rotation(position)

    *queries, k, v = project(blocks, attn_gain.reshape(1, -1), cosine, sine, w_held)
    guest_queries = [move_y(q) for q in queries]
    (cache,) = in_hbm(prefix_kv)
    seg_row, seg_col = segment.reshape(-1, 1), segment.reshape(1, -1)
    owns, guests, done = [], [], None
    owns.append(attend_own(mine, 0, queries[0], cache, own_there, k, v, seg_row, seg_col))
    for part in range(PARTS):
        q = after(guest_queries[part], owns[0][0])
        done = attend_guest(mine ^ 2, part, q, cache, guest_there)
        guests.append(move_y(done))
    for part in range(1, PARTS):
        q = after(queries[part], done, *guests[:-1])
        owns.append(attend_own(mine, part, q, cache, own_there, k, v, seg_row, seg_col))
    keep, send = join([o for o, _ in owns], [l for _, l in owns], guests, w_out)
    chip = keep + move_c(send).astype(F32)
    arrived = move_y(chip[dev:].astype(BF))
    resid, *messages = entry(
        mine, tokens, chip[:dev], arrived, moe_gain.reshape(1, -1), w_router, routes, CUTS
    )
    return mixture(group, resid, messages, (w_gate, w_up, w_down))


def solution(mesh):
    placed = (
        P(("tok", "head"), None),
        P("tok", None),
        P("tok", None),
        P("tok", "head", None, None),
        P(),
        P(None, None, "head"),
        P("head", None),
        P(),
        P(),
        P("tok", None, "head"),
        P("tok", None, "head"),
        P("tok", "head", None),
    )
    return jax.shard_map(
        on_device, mesh=mesh, in_specs=placed, out_specs=P(("tok", "head"), None), check_vma=False
    )
```

```python
import functools

import jax
import jax.numpy as jnp
from jax import lax
from jax.experimental import pallas as pl
from jax.experimental.pallas import tpu as pltpu
from jax.sharding import PartitionSpec as P

HD = 128
PREFIX = 2048
LANES = 128
LOG2E = 1.4426950408889634
CUTS = 2
PARTS = 2
rope_base = 10000.0
norm_eps = 1e-06
BF = jnp.bfloat16
F32 = jnp.float32


def params(mib):
    return pltpu.CompilerParams(vmem_limit_bytes=mib << 20)


def cost(flops, moved, exps=0):
    return pl.CostEstimate(flops=flops, bytes_accessed=moved, transcendentals=exps)


def whole(shape):
    return pl.BlockSpec(shape, lambda *_: (0,) * len(shape))


def swap(value, axis, bit):
    size = lax.axis_size(axis)
    return lax.ppermute(value, axis, [(i, i ^ bit) for i in range(size)])


move_x = functools.partial(swap, axis="tok", bit=1)
move_y = functools.partial(swap, axis="head", bit=2)
move_c = functools.partial(swap, axis="head", bit=1)


def from_z(value, k):
    size = lax.axis_size("tok")
    return lax.ppermute(value, "tok", [(i, (i - 2 * k) % size) for i in range(size)])


def to_z(value, k):
    return from_z(value, -k)


def in_hbm(*values):
    return [pltpu.with_memory_space_constraint(v, pltpu.HBM) for v in values]


def stage_kernel(who, kv, own, guest, sems):
    local = own.shape[2]
    some = kv.shape[1] // sems.shape[1]
    copies = []
    for i, (bit, target) in enumerate(((1, own), (3, guest))):
        cols = pl.ds(pl.multiple_of((who[0] ^ bit) * local, local), local)
        for j in range(sems.shape[1]):
            rows = pl.ds(j * some, some)
            copies.append(
                pltpu.make_async_copy(kv.at[0, rows, :, cols], target.at[rows], sems.at[i, j])
            )
    for copy in copies:
        copy.start()
    for copy in copies:
        copy.wait()


def stage(who, kv, local):
    depth = kv.shape[1]
    piece = jax.ShapeDtypeStruct((depth, 2, local), BF)
    return pl.pallas_call(
        stage_kernel,
        grid_spec=pltpu.PrefetchScalarGridSpec(
            num_scalar_prefetch=1,
            grid=(1,),
            in_specs=[pl.BlockSpec(memory_space=pltpu.HBM)],
            out_specs=[whole(piece.shape)] * 2,
            scratch_shapes=[pltpu.SemaphoreType.DMA((2, 4))],
        ),
        out_shape=[piece, piece],
        compiler_params=params(8),
        cost_estimate=cost(0, 8 * piece.size),
        name="stage",
    )(who, *in_hbm(kv))


def project_kernel(t0, t1, t2, t3, gain, cosine, sine, w, *refs):
    *queries, k, v, normed = refs
    rows = t0.shape[0]
    for i, ref in enumerate((t0, t1, t2, t3)):
        values = ref[...].astype(F32)
        mean_sq = jnp.mean(values * values, axis=-1, keepdims=True)
        scaled = values * lax.rsqrt(mean_sq + norm_eps) * gain[...]
        normed[pl.ds(i * rows, rows), :] = scaled.astype(BF)
    for part, outs in enumerate((queries, [k], [v])):
        out = jnp.dot(normed[...], w[part], preferred_element_type=F32)
        if part == 2:
            v[...] = out.astype(BF)
            continue
        heads = out.shape[1] // HD
        for h in range(heads):
            one = out[:, h * HD : (h + 1) * HD]
            turned = one * cosine[...] + pltpu.roll(one, HD // 2, 1) * sine[...]
            some = heads // len(outs)
            outs[h // some][:, h % some * HD : (h % some + 1) * HD] = turned.astype(BF)


def project(blocks, gain, cosine, sine, w):
    rows, width = blocks[0].shape
    total, local = 4 * rows, w.shape[2]
    widths = [local // PARTS] * PARTS + [local, local]
    return pl.pallas_call(
        project_kernel,
        out_shape=[jax.ShapeDtypeStruct((total, one), BF) for one in widths],
        in_specs=[pl.BlockSpec(memory_space=pltpu.VMEM)] * 8,
        out_specs=[pl.BlockSpec(memory_space=pltpu.VMEM)] * len(widths),
        scratch_shapes=[pltpu.VMEM((total, width), BF)],
        compiler_params=params(20),
        cost_estimate=cost(6 * total * width * local, 6 * width * local),
        name="project",
    )(*blocks, gain, cosine, sine, w)


def scores_of(q, keys):
    return lax.dot_general(q, keys, (((1,), (1,)), ((), ())), preferred_element_type=F32)


def attend_pieces(q, pieces):
    scale = HD**-0.5
    scores = []
    for keys, _, allowed in pieces:
        one = scores_of(q, keys)
        scores.append(one if allowed is None else jnp.where(allowed, one, -1e30))
    top = functools.reduce(jnp.maximum, [jnp.max(s, axis=-1, keepdims=True) for s in scores])
    mixed = 0.0
    for s, (_, values, _) in zip(scores, pieces):
        expo = jnp.exp2((s - top) * (scale * LOG2E)).astype(BF)
        wide = jnp.concatenate([values, jnp.ones(values.shape, BF)], axis=1)
        mixed = mixed + jnp.dot(expo, wide, preferred_element_type=F32)
    total = mixed[:, HD:]
    return mixed[:, :HD] / total, top * scale + jnp.log(total[:, :1])


def cached(kv_here, kv_there, cols):
    return [
        (kv_here[0, :, 0, cols], kv_here[0, :, 1, cols], None),
        (kv_there[:, 0, cols], kv_there[:, 1, cols], None),
    ]


def own_kernel(group, q, kv_here, kv_there, k, v, seg_row, seg_col, out, stats):
    same = seg_row[...] == seg_col[...]
    lane = lax.broadcasted_iota(jnp.int32, stats.shape, 1)
    levels = jnp.zeros(stats.shape, F32)
    for h in range(q.shape[1] // HD):
        cols = slice(h * HD, (h + 1) * HD)
        pieces = cached(kv_here, kv_there, cols) + [(k[:, cols], v[:, cols], same)]
        mixed, level = attend_pieces(q[:, cols], pieces)
        out[:, cols] = mixed
        levels = jnp.where(lane == h, level, levels)
    stats[...] = levels


def guest_kernel(group, q, kv_here, kv_there, out):
    local = out.shape[1] - LANES
    lane = lax.broadcasted_iota(jnp.int32, (out.shape[0], LANES), 1)
    tail = jnp.zeros(lane.shape, F32)
    for h in range(local // HD):
        cols = slice(h * HD, (h + 1) * HD)
        mixed, level = attend_pieces(q[:, cols], cached(kv_here, kv_there, cols))
        out[:, cols] = mixed.astype(BF)
        rest = jnp.broadcast_to(level, tail.shape)
        for i in range(3):
            piece = rest.astype(BF).astype(F32)
            tail = jnp.where(lane == 3 * h + i, piece, tail)
            rest = rest - piece
    out[:, local:] = tail.astype(BF)


def kv_specs(depth, some, part):
    return [
        pl.BlockSpec((1, depth, 2, some), lambda i, g: (0, 0, 0, g[0] * PARTS + part)),
        pl.BlockSpec((depth, 2, some), lambda i, g: (0, 0, part)),
    ]


def attend_own(group, part, q, kv, kv_there, k, v, seg_row, seg_col):
    rows, some = q.shape
    depth = kv.shape[1]
    block = pl.BlockSpec((rows, some), lambda i, g: (0, part))
    keys = 2 * depth + rows
    return pl.pallas_call(
        own_kernel,
        grid_spec=pltpu.PrefetchScalarGridSpec(
            num_scalar_prefetch=1,
            grid=(1,),
            in_specs=[whole((rows, some))]
            + kv_specs(depth, some, part)
            + [block, block, whole((rows, 1)), whole((1, rows))],
            out_specs=(whole((rows, some)), whole((rows, LANES))),
        ),
        out_shape=(
            jax.ShapeDtypeStruct((rows, some), F32),
            jax.ShapeDtypeStruct((rows, LANES), F32),
        ),
        compiler_params=params(20),
        cost_estimate=cost(4 * rows * keys * some, 4 * keys * some, rows * keys * some // HD),
        name="attend_own",
    )(group, q, kv, kv_there, k, v, seg_row, seg_col)


def attend_guest(group, part, q, kv, kv_there):
    rows, some = q.shape
    depth = kv.shape[1]
    keys = 2 * depth
    return pl.pallas_call(
        guest_kernel,
        grid_spec=pltpu.PrefetchScalarGridSpec(
            num_scalar_prefetch=1,
            grid=(1,),
            in_specs=[whole((rows, some))] + kv_specs(depth, some, part),
            out_specs=whole((rows, some + LANES)),
        ),
        out_shape=jax.ShapeDtypeStruct((rows, some + LANES), BF),
        compiler_params=params(20),
        cost_estimate=cost(4 * rows * keys * some, 4 * keys * some, rows * keys * some // HD),
        name="attend_guest",
    )(group, q, kv, kv_there)


def join_kernel(*refs):
    owns, levels, guests = (refs[i * PARTS : (i + 1) * PARTS] for i in range(3))
    w, keep, send = refs[3 * PARTS :]
    dev = keep.shape[0] // 2
    heads = []
    for own, stats, guest in zip(owns, levels, guests):
        some = own.shape[1]
        for h in range(some // HD):
            cols = slice(h * HD, (h + 1) * HD)
            first = stats[:, h : h + 1]
            start = some + 3 * h
            thirds = [guest[:, start + i : start + i + 1].astype(F32) for i in range(3)]
            second = functools.reduce(jnp.add, thirds)
            top = jnp.maximum(first, second)
            a, b = jnp.exp(first - top), jnp.exp(second - top)
            both = own[:, cols] * a + guest[:, cols].astype(F32) * b
            heads.append((both / (a + b)).astype(BF))
    mixed = jnp.concatenate(heads, axis=1)
    out = jnp.dot(mixed, w[...], preferred_element_type=F32)
    for i in range(2):
        keep[pl.ds(i * dev, dev), :] = out[2 * i * dev : (2 * i + 1) * dev]
        send[pl.ds(i * dev, dev), :] = out[(2 * i + 1) * dev : (2 * i + 2) * dev].astype(BF)


def join(owns, levels, guests, w):
    rows = owns[0].shape[0]
    local, width = w.shape
    return pl.pallas_call(
        join_kernel,
        out_shape=(
            jax.ShapeDtypeStruct((rows // 2, width), F32),
            jax.ShapeDtypeStruct((rows // 2, width), BF),
        ),
        compiler_params=params(20),
        cost_estimate=cost(2 * rows * local * width, 2 * local * width + 6 * rows * width // 2),
        name="join",
    )(*owns, *levels, *guests, w)


def entry_kernel(me, tokens, keep, arrived, gain, w_router, routes, resid, *messages):
    width = tokens.shape[1]
    experts = w_router.shape[1]
    values = tokens[...].astype(F32) + keep[...] + arrived[...].astype(F32)
    resid[...] = values
    mean_sq = jnp.mean(values * values, axis=-1, keepdims=True)
    normed = (values * lax.rsqrt(mean_sq + norm_eps) * gain[...]).astype(BF)
    logits = jnp.dot(normed, w_router[...], preferred_element_type=F32)
    lane = lax.broadcasted_iota(jnp.int32, logits.shape, 1)
    chosen = lane < 0
    for i in range(routes.shape[1]):
        chosen = chosen | (lane == routes[:, i : i + 1])
    logits = jnp.where(chosen, logits, -jnp.inf)
    expo = jnp.exp(logits - jnp.max(logits, axis=-1, keepdims=True))
    share = expo / jnp.sum(expo, axis=-1, keepdims=True)
    high = share.astype(BF)
    low = (share - high.astype(F32)).astype(BF)
    some = tokens.shape[0] // len(messages)
    for i, message in enumerate(messages):
        part = slice(i * some, (i + 1) * some)
        message[:, :width] = normed[part]
        message[:, width:] = jnp.zeros((some, LANES), BF)
        message[:, width : width + experts] = high[part]
        message[:, width + LANES // 2 : width + LANES // 2 + experts] = low[part]


def entry(me, tokens, keep, arrived, gain, w_router, routes, cuts):
    rows, width = tokens.shape
    some = rows // cuts
    experts, topk = w_router.shape[1], routes.shape[1]
    return pl.pallas_call(
        entry_kernel,
        grid_spec=pltpu.PrefetchScalarGridSpec(
            num_scalar_prefetch=1,
            grid=(1,),
            in_specs=[
                whole((rows, width)),
                whole((rows, width)),
                whole((rows, width)),
                whole((1, width)),
                whole((width, experts)),
                pl.BlockSpec((rows, topk), lambda i, m: (m[0], 0)),
            ],
            out_specs=(whole((rows, width)),) + (whole((some, width + LANES)),) * cuts,
        ),
        out_shape=(
            jax.ShapeDtypeStruct((rows, width), F32),
        )
        + (jax.ShapeDtypeStruct((some, width + LANES), BF),) * cuts,
        compiler_params=params(20),
        cost_estimate=cost(2 * rows * width * LANES, 12 * rows * width),
        name="entry",
    )(me, tokens, keep, arrived, gain, w_router, routes)


def expert_kernel(sizes, tile, group, *refs):
    count = len(sizes)
    pieces, (gate, up, down) = refs[:count], refs[count : count + 3]
    outs, (held, sems) = refs[count + 3 : -2], refs[-2:]
    experts, width = gate.shape[0], gate.shape[1]
    step = pl.program_id(0)

    @pl.when(step == 0)
    def _():
        start = 0
        for ref, size in zip(pieces, sizes):
            done = 0
            while done < size:
                take = min(size - done, tile - (start + done) % tile)
                pltpu.make_async_copy(
                    ref.at[pl.ds(done, take)],
                    held.at[pl.ds(start + done, take)],
                    sems.at[(start + done) // tile],
                ).start()
                done += take
            start += size

    here = pl.ds(pl.multiple_of(step * tile, tile), tile)
    pltpu.make_async_copy(held.at[here], held.at[here], sems.at[step]).wait()
    rows = held[here, :width]
    tail = held[here, width:].astype(F32)
    lane = lax.broadcasted_iota(jnp.int32, tail.shape, 1)
    result = None
    for e in range(experts):
        index = group[0] * experts + e
        hit = (lane == index) | (lane == index + LANES // 2)
        share = jnp.sum(jnp.where(hit, tail, 0.0), axis=1, keepdims=True)
        g = jnp.dot(rows, gate[e], preferred_element_type=F32)
        u = jnp.dot(rows, up[e], preferred_element_type=F32)
        act = (g * jax.nn.sigmoid(g) * u * share).astype(BF)
        one = jnp.dot(act, down[e], preferred_element_type=F32)
        result = one if result is None else result + one
    done = 0
    for out in outs:
        out[...] = result[done : done + out.shape[0]].astype(BF)
        done += out.shape[0]


def expert_part(group, pieces, weights, outs=1, most=512):
    gate = weights[0]
    sizes = [p.shape[0] for p in pieces]
    total = sum(sizes)
    tile = total if outs > 1 else next(t for t in range(most, 0, -64) if total % t == 0)
    wide, width = pieces[0].shape[1], gate.shape[1]
    some = tile // outs
    flops = 6 * total * gate.shape[0] * width * gate.shape[2]
    return pl.pallas_call(
        functools.partial(expert_kernel, sizes, tile),
        grid_spec=pltpu.PrefetchScalarGridSpec(
            num_scalar_prefetch=1,
            grid=(total // tile,),
            in_specs=[pl.BlockSpec(memory_space=pl.ANY)] * len(pieces)
            + [pl.BlockSpec(memory_space=pltpu.VMEM)] * 3,
            out_specs=(pl.BlockSpec((some, width), lambda i, g: (i, 0)),) * outs,
            scratch_shapes=[
                pltpu.VMEM((total, wide), BF),
                pltpu.SemaphoreType.DMA((total // tile,)),
            ],
        ),
        out_shape=(jax.ShapeDtypeStruct((total // outs, width), BF),) * outs,
        compiler_params=params(20 + (total >> 6)),
        cost_estimate=cost(flops, 4 * total * width + 6 * gate.size),
        name="experts",
    )(group, *pieces, *weights)


def add_bf(*values):
    return functools.reduce(jnp.add, [v.astype(F32) for v in values]).astype(BF)


def after(value, *others):
    return lax.optimization_barrier((value, *others))[0]


def join_rows(*values):
    return jnp.concatenate(values, axis=0)


def reduce_corner(kept, sent):
    total = add_bf(kept, move_c(sent))
    half = total.shape[0] // 2
    return move_y(total[:half]), move_x(total[half:])


def reduce_rest(total, got):
    n = total.shape[0] // 3
    half = n // 2
    rows = n // (lax.axis_size("tok") // 2)
    here, by_y, by_x = (total[i * n : (i + 1) * n] for i in range(3))
    first = add_bf(by_x[:half], got[0])
    to_x = join_rows(first[rows:], by_x[half:])
    to_y = join_rows(by_y[rows:half], add_bf(by_y[half:], got[1]))
    rest = add_bf(here[rows:], move_x(to_x), move_y(to_y))
    return rest, (here[:rows], by_y[:rows], first[:rows]), (to_x, to_y)


def hold_kernel(count, *refs):
    sources, targets, sems = refs[:count], refs[count : 2 * count], refs[-1]
    copies = []
    for i in range(count):
        some = sources[i].shape[1] // sems.shape[2]
        for e in range(sources[i].shape[0]):
            for j in range(sems.shape[2]):
                rows = pl.ds(j * some, some)
                copies.append(
                    pltpu.make_async_copy(
                        sources[i].at[e, rows], targets[i].at[e, rows], sems.at[i, e, j]
                    )
                )
    for copy in copies:
        copy.start()
    for copy in copies:
        copy.wait()


def hold(*values):
    count = len(values)
    return pl.pallas_call(
        functools.partial(hold_kernel, count),
        out_shape=[jax.ShapeDtypeStruct(v.shape, v.dtype) for v in values],
        in_specs=[pl.BlockSpec(memory_space=pltpu.HBM)] * count,
        out_specs=[pl.BlockSpec(memory_space=pltpu.VMEM)] * count,
        scratch_shapes=[pltpu.SemaphoreType.DMA((count, values[0].shape[0], 2))],
        compiler_params=params(1),
        cost_estimate=cost(0, sum(4 * v.size for v in values)),
        name="hold",
    )(*in_hbm(*values))


def mixture(group, resid, messages, weights):
    rows = messages[0].shape[0]
    depth = lax.axis_size("tok") // 2
    n, half = depth * rows, depth * rows // 2
    first, second = messages

    first_z = [from_z(first, k) for k in range(1, depth)]
    second = after(second, *first_z)
    second_z = [from_z(second, k) for k in range(1, depth)]
    here_a = join_rows(first, *first_z)
    y_a, x_a = move_y(here_a), move_x(here_a)
    held = hold(*after(weights, y_a, x_a))
    corner_a = [move_y(x_a[:half]), move_x(y_a[half:])]
    main_a = [here_a, y_a, x_a]
    their_main_a, their_corner_a = ([move_c(v) for v in values] for values in (main_a, corner_a))
    (sent_a,) = expert_part(group, their_main_a, held)
    here_b = join_rows(second, *after(second_z, *corner_a))
    leaving_b = here_b
    y_b, x_b = move_y(leaving_b), move_x(leaving_b)
    (kept_a,) = expert_part(group, after(main_a, sent_a), held)
    sent_corner, kept_corner = expert_part(
        group, after(their_corner_a, kept_a) + corner_a, held, 2
    )
    got_a = reduce_corner(after(kept_corner, y_b, x_b), sent_corner)

    corner_b = [move_y(x_b[:half]), move_x(y_b[half:])]
    main_b = [here_b, y_b, x_b]
    their_main_b = [move_c(v) for v in main_b]
    chip_a = add_bf(kept_a, move_c(sent_a))
    (sent_b,) = expert_part(group, after(their_main_b, sent_corner), held)
    (kept_b,) = expert_part(group, after(main_b, sent_b), held)
    corner_b = after(corner_b, kept_b)
    their_corner_b = [move_c(v) for v in corner_b]
    sent_corner, kept_corner = expert_part(group, their_corner_b + corner_b, held, 2)
    got_b = reduce_corner(kept_corner, sent_corner)
    rest_a, own_rows_a, _ = reduce_rest(chip_a, got_a)
    chip_b = add_bf(kept_b, move_c(sent_b))
    rest_b, own_rows_b, moving_b = reduce_rest(chip_b, got_b)

    def along_z(rest):
        parts = [rest[(k - 1) * rows : k * rows] for k in range(1, depth)]
        return [to_z(part, k) for k, part in zip(range(1, depth), parts)]

    landed_a = along_z(after(rest_a, *moving_b))
    landed_b = along_z(rest_b)
    here, to_y, to_x = (join_rows(u, v) for u, v in zip(own_rows_a, own_rows_b))
    to_y, to_x = after((to_y, to_x), rest_b)
    landed = [join_rows(u, v) for u, v in zip(landed_a, landed_b)]
    landed += [here, move_y(to_y), move_x(to_x)]
    return functools.reduce(jnp.add, [v.astype(F32) for v in landed], resid).astype(BF)


def request_layout(lengths_row, index):
    ends = jnp.cumsum(lengths_row)
    passed = (index[:, None] >= ends[None, :]).astype(jnp.int32)
    segment = jnp.sum(passed, axis=1)
    offset = index - jnp.sum(passed * lengths_row[None, :], axis=1)
    return segment, PREFIX + offset


def rotation(position):
    half = HD // 2
    freq = rope_base ** (-(jnp.arange(half).astype(F32) * 2.0) / HD)
    angle = position[:, None].astype(F32) * freq[None, :]
    cosine, sine = jnp.cos(angle), jnp.sin(angle)
    return jnp.concatenate([cosine, cosine], 1), jnp.concatenate([-sine, sine], 1)


def on_device(
    tokens, lengths, routes, prefix_kv, attn_gain, w_qkv, w_out, moe_gain, w_router, w_gate, w_up, w_down
):
    dev, width = tokens.shape
    local = w_qkv.shape[2]
    me = lax.axis_index("head")
    group = lax.axis_index("tok").astype(jnp.int32).reshape(1)

    by_c, by_y = move_c(tokens), move_y(tokens)
    mine = me.astype(jnp.int32).reshape(1)
    own_there, guest_there = stage(mine, prefix_kv, local)
    (w_held,) = hold(jnp.transpose(w_qkv, (1, 0, 2)))
    blocks = [tokens, by_c, by_y, move_c(after(by_y, w_held, guest_there))]

    own_there, guest_there = move_c(own_there), move_c(guest_there)

    index = ((me ^ jnp.arange(4))[:, None] * dev + jnp.arange(dev)[None, :]).reshape(-1)
    segment, position = request_layout(lengths[0], index)
    cosine, sine = rotation(position)

    *queries, k, v = project(blocks, attn_gain.reshape(1, -1), cosine, sine, w_held)
    guest_queries = [move_y(q) for q in queries]
    (cache,) = in_hbm(prefix_kv)
    seg_row, seg_col = segment.reshape(-1, 1), segment.reshape(1, -1)
    owns, guests, done = [], [], None
    owns.append(attend_own(mine, 0, queries[0], cache, own_there, k, v, seg_row, seg_col))
    for part in range(PARTS):
        q = after(guest_queries[part], owns[0][0])
        done = attend_guest(mine ^ 2, part, q, cache, guest_there)
        guests.append(move_y(done))
    for part in range(1, PARTS):
        q = after(queries[part], done, *guests[:-1])
        owns.append(attend_own(mine, part, q, cache, own_there, k, v, seg_row, seg_col))
    keep, send = join([o for o, _ in owns], [l for _, l in owns], guests, w_out)
    chip = keep + move_c(send).astype(F32)
    arrived = move_y(chip[dev:].astype(BF))
    resid, *messages = entry(
        mine, tokens, chip[:dev], arrived, moe_gain.reshape(1, -1), w_router, routes, CUTS
    )
    return mixture(group, resid, messages, (w_gate, w_up, w_down))


def solution(mesh):
    placed = (
        P(("tok", "head"), None),
        P("tok", None),
        P("tok", None),
        P("tok", "head", None, None),
        P(),
        P(None, None, "head"),
        P("head", None),
        P(),
        P(),
        P("tok", None, "head"),
        P("tok", None, "head"),
        P("tok", "head", None),
    )
    return jax.shard_map(
        on_device, mesh=mesh, in_specs=placed, out_specs=P(("tok", "head"), None), check_vma=False
    )
```

```python
import functools

import jax
import jax.numpy as jnp
from jax import lax
from jax.experimental import pallas as pl
from jax.experimental.pallas import tpu as pltpu
from jax.sharding import PartitionSpec as P

HD = 128
PREFIX = 2048
LANES = 128
LOG2E = 1.4426950408889634
CUTS = 2
PARTS = 2
rope_base = 10000.0
norm_eps = 1e-06
BF = jnp.bfloat16
F32 = jnp.float32


def params(mib):
    return pltpu.CompilerParams(vmem_limit_bytes=mib << 20)


def cost(flops, moved, exps=0):
    return pl.CostEstimate(flops=flops, bytes_accessed=moved, transcendentals=exps)


def whole(shape):
    return pl.BlockSpec(shape, lambda *_: (0,) * len(shape))


def swap(value, axis, bit):
    size = lax.axis_size(axis)
    return lax.ppermute(value, axis, [(i, i ^ bit) for i in range(size)])


move_x = functools.partial(swap, axis="tok", bit=1)
move_y = functools.partial(swap, axis="head", bit=2)
move_c = functools.partial(swap, axis="head", bit=1)


def from_z(value, k):
    size = lax.axis_size("tok")
    return lax.ppermute(value, "tok", [(i, (i - 2 * k) % size) for i in range(size)])


def to_z(value, k):
    return from_z(value, -k)


def in_hbm(*values):
    return [pltpu.with_memory_space_constraint(v, pltpu.HBM) for v in values]


def stage_kernel(who, kv, own, guest, sems):
    local = own.shape[2]
    some = kv.shape[1] // sems.shape[1]
    copies = []
    for i, (bit, target) in enumerate(((1, own), (3, guest))):
        cols = pl.ds(pl.multiple_of((who[0] ^ bit) * local, local), local)
        for j in range(sems.shape[1]):
            rows = pl.ds(j * some, some)
            copies.append(
                pltpu.make_async_copy(kv.at[0, rows, :, cols], target.at[rows], sems.at[i, j])
            )
    for copy in copies:
        copy.start()
    for copy in copies:
        copy.wait()


def stage(who, kv, local):
    depth = kv.shape[1]
    piece = jax.ShapeDtypeStruct((depth, 2, local), BF)
    return pl.pallas_call(
        stage_kernel,
        grid_spec=pltpu.PrefetchScalarGridSpec(
            num_scalar_prefetch=1,
            grid=(1,),
            in_specs=[pl.BlockSpec(memory_space=pltpu.HBM)],
            out_specs=[whole(piece.shape)] * 2,
            scratch_shapes=[pltpu.SemaphoreType.DMA((2, 4))],
        ),
        out_shape=[piece, piece],
        compiler_params=params(8),
        cost_estimate=cost(0, 8 * piece.size),
        name="stage",
    )(who, *in_hbm(kv))


def project_kernel(t0, t1, t2, t3, gain, cosine, sine, w, *refs):
    *queries, k, v, normed = refs
    rows = t0.shape[0]
    for i, ref in enumerate((t0, t1, t2, t3)):
        values = ref[...].astype(F32)
        mean_sq = jnp.mean(values * values, axis=-1, keepdims=True)
        scaled = values * lax.rsqrt(mean_sq + norm_eps) * gain[...]
        normed[pl.ds(i * rows, rows), :] = scaled.astype(BF)
    for part, outs in enumerate((queries, [k], [v])):
        out = jnp.dot(normed[...], w[part], preferred_element_type=F32)
        if part == 2:
            v[...] = out.astype(BF)
            continue
        heads = out.shape[1] // HD
        for h in range(heads):
            one = out[:, h * HD : (h + 1) * HD]
            turned = one * cosine[...] + pltpu.roll(one, HD // 2, 1) * sine[...]
            some = heads // len(outs)
            outs[h // some][:, h % some * HD : (h % some + 1) * HD] = turned.astype(BF)


def project(blocks, gain, cosine, sine, w):
    rows, width = blocks[0].shape
    total, local = 4 * rows, w.shape[2]
    widths = [local // PARTS] * PARTS + [local, local]
    return pl.pallas_call(
        project_kernel,
        out_shape=[jax.ShapeDtypeStruct((total, one), BF) for one in widths],
        in_specs=[pl.BlockSpec(memory_space=pltpu.VMEM)] * 8,
        out_specs=[pl.BlockSpec(memory_space=pltpu.VMEM)] * len(widths),
        scratch_shapes=[pltpu.VMEM((total, width), BF)],
        compiler_params=params(20),
        cost_estimate=cost(6 * total * width * local, 6 * width * local),
        name="project",
    )(*blocks, gain, cosine, sine, w)


def scores_of(q, keys):
    return lax.dot_general(q, keys, (((1,), (1,)), ((), ())), preferred_element_type=F32)


def attend_pieces(q, pieces):
    scale = HD**-0.5
    scores = []
    for keys, _, allowed in pieces:
        one = scores_of(q, keys)
        scores.append(one if allowed is None else jnp.where(allowed, one, -1e30))
    top = functools.reduce(jnp.maximum, [jnp.max(s, axis=-1, keepdims=True) for s in scores])
    mixed = 0.0
    for s, (_, values, _) in zip(scores, pieces):
        expo = jnp.exp2((s - top) * (scale * LOG2E)).astype(BF)
        wide = jnp.concatenate([values, jnp.ones(values.shape, BF)], axis=1)
        mixed = mixed + jnp.dot(expo, wide, preferred_element_type=F32)
    total = mixed[:, HD:]
    return mixed[:, :HD] / total, top * scale + jnp.log(total[:, :1])


def cached(kv_here, kv_there, cols):
    return [
        (kv_here[0, :, 0, cols], kv_here[0, :, 1, cols], None),
        (kv_there[:, 0, cols], kv_there[:, 1, cols], None),
    ]


def own_kernel(group, q, kv_here, kv_there, k, v, seg_row, seg_col, out, stats):
    same = seg_row[...] == seg_col[...]
    lane = lax.broadcasted_iota(jnp.int32, stats.shape, 1)
    levels = jnp.zeros(stats.shape, F32)
    for h in range(q.shape[1] // HD):
        cols = slice(h * HD, (h + 1) * HD)
        pieces = cached(kv_here, kv_there, cols) + [(k[:, cols], v[:, cols], same)]
        mixed, level = attend_pieces(q[:, cols], pieces)
        out[:, cols] = mixed
        levels = jnp.where(lane == h, level, levels)
    stats[...] = levels


def guest_kernel(group, q, kv_here, kv_there, out):
    local = out.shape[1] - LANES
    lane = lax.broadcasted_iota(jnp.int32, (out.shape[0], LANES), 1)
    tail = jnp.zeros(lane.shape, F32)
    for h in range(local // HD):
        cols = slice(h * HD, (h + 1) * HD)
        mixed, level = attend_pieces(q[:, cols], cached(kv_here, kv_there, cols))
        out[:, cols] = mixed.astype(BF)
        rest = jnp.broadcast_to(level, tail.shape)
        for i in range(3):
            piece = rest.astype(BF).astype(F32)
            tail = jnp.where(lane == 3 * h + i, piece, tail)
            rest = rest - piece
    out[:, local:] = tail.astype(BF)


def kv_specs(depth, some, part):
    return [
        pl.BlockSpec((1, depth, 2, some), lambda i, g: (0, 0, 0, g[0] * PARTS + part)),
        pl.BlockSpec((depth, 2, some), lambda i, g: (0, 0, part)),
    ]


def attend_own(group, part, q, kv, kv_there, k, v, seg_row, seg_col):
    rows, some = q.shape
    depth = kv.shape[1]
    block = pl.BlockSpec((rows, some), lambda i, g: (0, part))
    keys = 2 * depth + rows
    return pl.pallas_call(
        own_kernel,
        grid_spec=pltpu.PrefetchScalarGridSpec(
            num_scalar_prefetch=1,
            grid=(1,),
            in_specs=[whole((rows, some))]
            + kv_specs(depth, some, part)
            + [block, block, whole((rows, 1)), whole((1, rows))],
            out_specs=(whole((rows, some)), whole((rows, LANES))),
        ),
        out_shape=(
            jax.ShapeDtypeStruct((rows, some), F32),
            jax.ShapeDtypeStruct((rows, LANES), F32),
        ),
        compiler_params=params(20),
        cost_estimate=cost(4 * rows * keys * some, 4 * keys * some, rows * keys * some // HD),
        name="attend_own",
    )(group, q, kv, kv_there, k, v, seg_row, seg_col)


def attend_guest(group, part, q, kv, kv_there):
    rows, some = q.shape
    depth = kv.shape[1]
    keys = 2 * depth
    return pl.pallas_call(
        guest_kernel,
        grid_spec=pltpu.PrefetchScalarGridSpec(
            num_scalar_prefetch=1,
            grid=(1,),
            in_specs=[whole((rows, some))] + kv_specs(depth, some, part),
            out_specs=whole((rows, some + LANES)),
        ),
        out_shape=jax.ShapeDtypeStruct((rows, some + LANES), BF),
        compiler_params=params(20),
        cost_estimate=cost(4 * rows * keys * some, 4 * keys * some, rows * keys * some // HD),
        name="attend_guest",
    )(group, q, kv, kv_there)


def join_kernel(*refs):
    owns, levels, guests = (refs[i * PARTS : (i + 1) * PARTS] for i in range(3))
    w, keep, send = refs[3 * PARTS :]
    dev = keep.shape[0] // 2
    heads = []
    for own, stats, guest in zip(owns, levels, guests):
        some = own.shape[1]
        for h in range(some // HD):
            cols = slice(h * HD, (h + 1) * HD)
            first = stats[:, h : h + 1]
            start = some + 3 * h
            thirds = [guest[:, start + i : start + i + 1].astype(F32) for i in range(3)]
            second = functools.reduce(jnp.add, thirds)
            top = jnp.maximum(first, second)
            a, b = jnp.exp(first - top), jnp.exp(second - top)
            both = own[:, cols] * a + guest[:, cols].astype(F32) * b
            heads.append((both / (a + b)).astype(BF))
    mixed = jnp.concatenate(heads, axis=1)
    out = jnp.dot(mixed, w[...], preferred_element_type=F32)
    for i in range(2):
        keep[pl.ds(i * dev, dev), :] = out[2 * i * dev : (2 * i + 1) * dev]
        send[pl.ds(i * dev, dev), :] = out[(2 * i + 1) * dev : (2 * i + 2) * dev].astype(BF)


def join(owns, levels, guests, w):
    rows = owns[0].shape[0]
    local, width = w.shape
    return pl.pallas_call(
        join_kernel,
        out_shape=(
            jax.ShapeDtypeStruct((rows // 2, width), F32),
            jax.ShapeDtypeStruct((rows // 2, width), BF),
        ),
        compiler_params=params(20),
        cost_estimate=cost(2 * rows * local * width, 2 * local * width + 6 * rows * width // 2),
        name="join",
    )(*owns, *levels, *guests, w)


def entry_kernel(me, tokens, keep, arrived, gain, w_router, routes, resid, *messages):
    width = tokens.shape[1]
    experts = w_router.shape[1]
    values = tokens[...].astype(F32) + keep[...] + arrived[...].astype(F32)
    resid[...] = values
    mean_sq = jnp.mean(values * values, axis=-1, keepdims=True)
    normed = (values * lax.rsqrt(mean_sq + norm_eps) * gain[...]).astype(BF)
    logits = jnp.dot(normed, w_router[...], preferred_element_type=F32)
    lane = lax.broadcasted_iota(jnp.int32, logits.shape, 1)
    chosen = lane < 0
    for i in range(routes.shape[1]):
        chosen = chosen | (lane == routes[:, i : i + 1])
    logits = jnp.where(chosen, logits, -jnp.inf)
    expo = jnp.exp(logits - jnp.max(logits, axis=-1, keepdims=True))
    share = expo / jnp.sum(expo, axis=-1, keepdims=True)
    high = share.astype(BF)
    low = (share - high.astype(F32)).astype(BF)
    some = tokens.shape[0] // len(messages)
    for i, message in enumerate(messages):
        part = slice(i * some, (i + 1) * some)
        message[:, :width] = normed[part]
        message[:, width:] = jnp.zeros((some, LANES), BF)
        message[:, width : width + experts] = high[part]
        message[:, width + LANES // 2 : width + LANES // 2 + experts] = low[part]


def entry(me, tokens, keep, arrived, gain, w_router, routes, cuts):
    rows, width = tokens.shape
    some = rows // cuts
    experts, topk = w_router.shape[1], routes.shape[1]
    return pl.pallas_call(
        entry_kernel,
        grid_spec=pltpu.PrefetchScalarGridSpec(
            num_scalar_prefetch=1,
            grid=(1,),
            in_specs=[
                whole((rows, width)),
                whole((rows, width)),
                whole((rows, width)),
                whole((1, width)),
                whole((width, experts)),
                pl.BlockSpec((rows, topk), lambda i, m: (m[0], 0)),
            ],
            out_specs=(whole((rows, width)),) + (whole((some, width + LANES)),) * cuts,
        ),
        out_shape=(
            jax.ShapeDtypeStruct((rows, width), F32),
        )
        + (jax.ShapeDtypeStruct((some, width + LANES), BF),) * cuts,
        compiler_params=params(20),
        cost_estimate=cost(2 * rows * width * LANES, 12 * rows * width),
        name="entry",
    )(me, tokens, keep, arrived, gain, w_router, routes)


def expert_kernel(sizes, tile, group, *refs):
    count = len(sizes)
    pieces, (gate, up, down) = refs[:count], refs[count : count + 3]
    outs, (held, sems) = refs[count + 3 : -2], refs[-2:]
    experts, width = gate.shape[0], gate.shape[1]
    step = pl.program_id(0)

    @pl.when(step == 0)
    def _():
        start = 0
        for ref, size in zip(pieces, sizes):
            done = 0
            while done < size:
                take = min(size - done, tile - (start + done) % tile)
                pltpu.make_async_copy(
                    ref.at[pl.ds(done, take)],
                    held.at[pl.ds(start + done, take)],
                    sems.at[(start + done) // tile],
                ).start()
                done += take
            start += size

    here = pl.ds(pl.multiple_of(step * tile, tile), tile)
    pltpu.make_async_copy(held.at[here], held.at[here], sems.at[step]).wait()
    rows = held[here, :width]
    tail = held[here, width:].astype(F32)
    lane = lax.broadcasted_iota(jnp.int32, tail.shape, 1)
    result = None
    for e in range(experts):
        index = group[0] * experts + e
        hit = (lane == index) | (lane == index + LANES // 2)
        share = jnp.sum(jnp.where(hit, tail, 0.0), axis=1, keepdims=True)
        g = jnp.dot(rows, gate[e], preferred_element_type=F32)
        u = jnp.dot(rows, up[e], preferred_element_type=F32)
        act = (g * jax.nn.sigmoid(g) * u * share).astype(BF)
        one = jnp.dot(act, down[e], preferred_element_type=F32)
        result = one if result is None else result + one
    done = 0
    for out in outs:
        out[...] = result[done : done + out.shape[0]].astype(BF)
        done += out.shape[0]


def expert_part(group, pieces, weights, outs=1, most=512):
    gate = weights[0]
    sizes = [p.shape[0] for p in pieces]
    total = sum(sizes)
    tile = total if outs > 1 else next(t for t in range(most, 0, -64) if total % t == 0)
    wide, width = pieces[0].shape[1], gate.shape[1]
    some = tile // outs
    flops = 6 * total * gate.shape[0] * width * gate.shape[2]
    return pl.pallas_call(
        functools.partial(expert_kernel, sizes, tile),
        grid_spec=pltpu.PrefetchScalarGridSpec(
            num_scalar_prefetch=1,
            grid=(total // tile,),
            in_specs=[pl.BlockSpec(memory_space=pl.ANY)] * len(pieces)
            + [pl.BlockSpec(memory_space=pltpu.VMEM)] * 3,
            out_specs=(pl.BlockSpec((some, width), lambda i, g: (i, 0)),) * outs,
            scratch_shapes=[
                pltpu.VMEM((total, wide), BF),
                pltpu.SemaphoreType.DMA((total // tile,)),
            ],
        ),
        out_shape=(jax.ShapeDtypeStruct((total // outs, width), BF),) * outs,
        compiler_params=params(20 + (total >> 6)),
        cost_estimate=cost(flops, 4 * total * width + 6 * gate.size),
        name="experts",
    )(group, *pieces, *weights)


def add_bf(*values):
    return functools.reduce(jnp.add, [v.astype(F32) for v in values]).astype(BF)


def after(value, *others):
    return lax.optimization_barrier((value, *others))[0]


def join_rows(*values):
    return jnp.concatenate(values, axis=0)


def reduce_corner(kept, sent):
    total = add_bf(kept, move_c(sent))
    half = total.shape[0] // 2
    return move_y(total[:half]), move_x(total[half:])


def reduce_rest(total, got):
    n = total.shape[0] // 3
    half = n // 2
    rows = n // (lax.axis_size("tok") // 2)
    here, by_y, by_x = (total[i * n : (i + 1) * n] for i in range(3))
    first = add_bf(by_x[:half], got[0])
    to_x = join_rows(first[rows:], by_x[half:])
    to_y = join_rows(by_y[rows:half], add_bf(by_y[half:], got[1]))
    rest = add_bf(here[rows:], move_x(to_x), move_y(to_y))
    return rest, (here[:rows], by_y[:rows], first[:rows]), (to_x, to_y)


def hold_kernel(count, *refs):
    sources, targets, sems = refs[:count], refs[count : 2 * count], refs[-1]
    copies = []
    for i in range(count):
        some = sources[i].shape[1] // sems.shape[2]
        for e in range(sources[i].shape[0]):
            for j in range(sems.shape[2]):
                rows = pl.ds(j * some, some)
                copies.append(
                    pltpu.make_async_copy(
                        sources[i].at[e, rows], targets[i].at[e, rows], sems.at[i, e, j]
                    )
                )
    for copy in copies:
        copy.start()
    for copy in copies:
        copy.wait()


def hold(*values):
    count = len(values)
    return pl.pallas_call(
        functools.partial(hold_kernel, count),
        out_shape=[jax.ShapeDtypeStruct(v.shape, v.dtype) for v in values],
        in_specs=[pl.BlockSpec(memory_space=pltpu.HBM)] * count,
        out_specs=[pl.BlockSpec(memory_space=pltpu.VMEM)] * count,
        scratch_shapes=[pltpu.SemaphoreType.DMA((count, values[0].shape[0], 2))],
        compiler_params=params(1),
        cost_estimate=cost(0, sum(4 * v.size for v in values)),
        name="hold",
    )(*in_hbm(*values))


def mixture(group, resid, messages, weights):
    rows = messages[0].shape[0]
    depth = lax.axis_size("tok") // 2
    n, half = depth * rows, depth * rows // 2
    first, second = messages

    first_z = [from_z(first, k) for k in range(1, depth)]
    second = after(second, *first_z)
    second_z = [from_z(second, k) for k in range(1, depth)]
    here_a = join_rows(first, *first_z)
    y_a, x_a = move_y(here_a), move_x(here_a)
    held = hold(*after(weights, y_a, x_a))
    corner_a = [move_y(x_a[:half]), move_x(y_a[half:])]
    main_a = [here_a, y_a, x_a]
    their_main_a, their_corner_a = ([move_c(v) for v in values] for values in (main_a, corner_a))
    (sent_a,) = expert_part(group, their_main_a, held)
    here_b = join_rows(second, *after(second_z, *corner_a))
    leaving_b = here_b
    y_b, x_b = move_y(leaving_b), move_x(leaving_b)
    (kept_a,) = expert_part(group, after(main_a, sent_a), held)
    sent_corner, kept_corner = expert_part(
        group, after(their_corner_a, kept_a) + corner_a, held, 2
    )
    got_a = reduce_corner(after(kept_corner, y_b, x_b), sent_corner)

    corner_b = [move_y(x_b[:half]), move_x(y_b[half:])]
    main_b = [here_b, y_b, x_b]
    their_main_b = [move_c(v) for v in main_b]
    chip_a = add_bf(kept_a, move_c(sent_a))
    (sent_b,) = expert_part(group, after(their_main_b, sent_corner), held)
    (kept_b,) = expert_part(group, after(main_b, sent_b), held)
    corner_b = after(corner_b, kept_b)
    their_corner_b = [move_c(v) for v in corner_b]
    sent_corner, kept_corner = expert_part(group, their_corner_b + corner_b, held, 2)
    got_b = reduce_corner(kept_corner, sent_corner)
    chip_b = add_bf(kept_b, move_c(sent_b))
    rest_a, own_rows_a, _ = reduce_rest(chip_a, after(got_a, chip_b))
    rest_b, own_rows_b, moving_b = reduce_rest(chip_b, got_b)

    def along_z(rest):
        parts = [rest[(k - 1) * rows : k * rows] for k in range(1, depth)]
        return [to_z(part, k) for k, part in zip(range(1, depth), parts)]

    landed_a = along_z(after(rest_a, *moving_b))
    landed_b = along_z(rest_b)
    here, to_y, to_x = (join_rows(u, v) for u, v in zip(own_rows_a, own_rows_b))
    to_y, to_x = after((to_y, to_x), rest_b)
    landed = [join_rows(u, v) for u, v in zip(landed_a, landed_b)]
    landed += [here, move_y(to_y), move_x(to_x)]
    return functools.reduce(jnp.add, [v.astype(F32) for v in landed], resid).astype(BF)


def request_layout(lengths_row, index):
    ends = jnp.cumsum(lengths_row)
    passed = (index[:, None] >= ends[None, :]).astype(jnp.int32)
    segment = jnp.sum(passed, axis=1)
    offset = index - jnp.sum(passed * lengths_row[None, :], axis=1)
    return segment, PREFIX + offset


def rotation(position):
    half = HD // 2
    freq = rope_base ** (-(jnp.arange(half).astype(F32) * 2.0) / HD)
    angle = position[:, None].astype(F32) * freq[None, :]
    cosine, sine = jnp.cos(angle), jnp.sin(angle)
    return jnp.concatenate([cosine, cosine], 1), jnp.concatenate([-sine, sine], 1)


def on_device(
    tokens, lengths, routes, prefix_kv, attn_gain, w_qkv, w_out, moe_gain, w_router, w_gate, w_up, w_down
):
    dev, width = tokens.shape
    local = w_qkv.shape[2]
    me = lax.axis_index("head")
    group = lax.axis_index("tok").astype(jnp.int32).reshape(1)

    by_c, by_y = move_c(tokens), move_y(tokens)
    mine = me.astype(jnp.int32).reshape(1)
    own_there, guest_there = stage(mine, prefix_kv, local)
    (w_held,) = hold(jnp.transpose(w_qkv, (1, 0, 2)))
    blocks = [tokens, by_c, by_y, move_c(after(by_y, w_held, guest_there))]

    own_there, guest_there = move_c(own_there), move_c(guest_there)

    index = ((me ^ jnp.arange(4))[:, None] * dev + jnp.arange(dev)[None, :]).reshape(-1)
    segment, position = request_layout(lengths[0], index)
    cosine, sine = rotation(position)

    *queries, k, v = project(blocks, attn_gain.reshape(1, -1), cosine, sine, w_held)
    guest_queries = [move_y(q) for q in queries]
    (cache,) = in_hbm(prefix_kv)
    seg_row, seg_col = segment.reshape(-1, 1), segment.reshape(1, -1)
    owns, guests, done = [], [], None
    owns.append(attend_own(mine, 0, queries[0], cache, own_there, k, v, seg_row, seg_col))
    for part in range(PARTS):
        q = after(guest_queries[part], owns[0][0])
        done = attend_guest(mine ^ 2, part, q, cache, guest_there)
        guests.append(move_y(done))
    for part in range(1, PARTS):
        q = after(queries[part], done, *guests[:-1])
        owns.append(attend_own(mine, part, q, cache, own_there, k, v, seg_row, seg_col))
    keep, send = join([o for o, _ in owns], [l for _, l in owns], guests, w_out)
    chip = keep + move_c(send).astype(F32)
    arrived = move_y(chip[dev:].astype(BF))
    resid, *messages = entry(
        mine, tokens, chip[:dev], arrived, moe_gain.reshape(1, -1), w_router, routes, CUTS
    )
    return mixture(group, resid, messages, (w_gate, w_up, w_down))


def solution(mesh):
    placed = (
        P(("tok", "head"), None),
        P("tok", None),
        P("tok", None),
        P("tok", "head", None, None),
        P(),
        P(None, None, "head"),
        P("head", None),
        P(),
        P(),
        P("tok", None, "head"),
        P("tok", None, "head"),
        P("tok", "head", None),
    )
    return jax.shard_map(
        on_device, mesh=mesh, in_specs=placed, out_specs=P(("tok", "head"), None), check_vma=False
    )
```

```python
import functools

import jax
import jax.numpy as jnp
from jax import lax
from jax.experimental import pallas as pl
from jax.experimental.pallas import tpu as pltpu
from jax.sharding import PartitionSpec as P

HD = 128
PREFIX = 2048
LANES = 128
LOG2E = 1.4426950408889634
CUTS = 2
PARTS = 2
rope_base = 10000.0
norm_eps = 1e-06
BF = jnp.bfloat16
F32 = jnp.float32


def params(mib):
    return pltpu.CompilerParams(vmem_limit_bytes=mib << 20)


def cost(flops, moved, exps=0):
    return pl.CostEstimate(flops=flops, bytes_accessed=moved, transcendentals=exps)


def whole(shape):
    return pl.BlockSpec(shape, lambda *_: (0,) * len(shape))


def swap(value, axis, bit):
    size = lax.axis_size(axis)
    return lax.ppermute(value, axis, [(i, i ^ bit) for i in range(size)])


move_x = functools.partial(swap, axis="tok", bit=1)
move_y = functools.partial(swap, axis="head", bit=2)
move_c = functools.partial(swap, axis="head", bit=1)


def from_z(value, k):
    size = lax.axis_size("tok")
    return lax.ppermute(value, "tok", [(i, (i - 2 * k) % size) for i in range(size)])


def to_z(value, k):
    return from_z(value, -k)


def in_hbm(*values):
    return [pltpu.with_memory_space_constraint(v, pltpu.HBM) for v in values]


def stage_kernel(who, kv, own, guest, sems):
    local = own.shape[2]
    some = kv.shape[1] // sems.shape[1]
    copies = []
    for i, (bit, target) in enumerate(((1, own), (3, guest))):
        cols = pl.ds(pl.multiple_of((who[0] ^ bit) * local, local), local)
        for j in range(sems.shape[1]):
            rows = pl.ds(j * some, some)
            copies.append(
                pltpu.make_async_copy(kv.at[0, rows, :, cols], target.at[rows], sems.at[i, j])
            )
    for copy in copies:
        copy.start()
    for copy in copies:
        copy.wait()


def stage(who, kv, local):
    depth = kv.shape[1]
    piece = jax.ShapeDtypeStruct((depth, 2, local), BF)
    return pl.pallas_call(
        stage_kernel,
        grid_spec=pltpu.PrefetchScalarGridSpec(
            num_scalar_prefetch=1,
            grid=(1,),
            in_specs=[pl.BlockSpec(memory_space=pltpu.HBM)],
            out_specs=[whole(piece.shape)] * 2,
            scratch_shapes=[pltpu.SemaphoreType.DMA((2, 4))],
        ),
        out_shape=[piece, piece],
        compiler_params=params(8),
        cost_estimate=cost(0, 8 * piece.size),
        name="stage",
    )(who, *in_hbm(kv))


def project_kernel(t0, t1, t2, t3, gain, cosine, sine, w, *refs):
    *queries, k, v, normed = refs
    rows = t0.shape[0]
    for i, ref in enumerate((t0, t1, t2, t3)):
        values = ref[...].astype(F32)
        mean_sq = jnp.mean(values * values, axis=-1, keepdims=True)
        scaled = values * lax.rsqrt(mean_sq + norm_eps) * gain[...]
        normed[pl.ds(i * rows, rows), :] = scaled.astype(BF)
    for part, outs in enumerate((queries, [k], [v])):
        out = jnp.dot(normed[...], w[part], preferred_element_type=F32)
        if part == 2:
            v[...] = out.astype(BF)
            continue
        heads = out.shape[1] // HD
        for h in range(heads):
            one = out[:, h * HD : (h + 1) * HD]
            turned = one * cosine[...] + pltpu.roll(one, HD // 2, 1) * sine[...]
            some = heads // len(outs)
            outs[h // some][:, h % some * HD : (h % some + 1) * HD] = turned.astype(BF)


def project(blocks, gain, cosine, sine, w):
    rows, width = blocks[0].shape
    total, local = 4 * rows, w.shape[2]
    widths = [local // PARTS] * PARTS + [local, local]
    return pl.pallas_call(
        project_kernel,
        out_shape=[jax.ShapeDtypeStruct((total, one), BF) for one in widths],
        in_specs=[pl.BlockSpec(memory_space=pltpu.VMEM)] * 8,
        out_specs=[pl.BlockSpec(memory_space=pltpu.VMEM)] * len(widths),
        scratch_shapes=[pltpu.VMEM((total, width), BF)],
        compiler_params=params(20),
        cost_estimate=cost(6 * total * width * local, 6 * width * local),
        name="project",
    )(*blocks, gain, cosine, sine, w)


def scores_of(q, keys):
    return lax.dot_general(q, keys, (((1,), (1,)), ((), ())), preferred_element_type=F32)


def attend_pieces(q, pieces):
    scale = HD**-0.5
    scores = []
    for keys, _, allowed in pieces:
        one = scores_of(q, keys)
        scores.append(one if allowed is None else jnp.where(allowed, one, -1e30))
    top = functools.reduce(jnp.maximum, [jnp.max(s, axis=-1, keepdims=True) for s in scores])
    mixed = 0.0
    for s, (_, values, _) in zip(scores, pieces):
        expo = jnp.exp2((s - top) * (scale * LOG2E)).astype(BF)
        wide = jnp.concatenate([values, jnp.ones(values.shape, BF)], axis=1)
        mixed = mixed + jnp.dot(expo, wide, preferred_element_type=F32)
    total = mixed[:, HD:]
    return mixed[:, :HD] / total, top * scale + jnp.log(total[:, :1])


def cached(kv_here, kv_there, cols):
    return [
        (kv_here[0, :, 0, cols], kv_here[0, :, 1, cols], None),
        (kv_there[:, 0, cols], kv_there[:, 1, cols], None),
    ]


def own_kernel(group, q, kv_here, kv_there, k, v, seg_row, seg_col, out, stats):
    same = seg_row[...] == seg_col[...]
    lane = lax.broadcasted_iota(jnp.int32, stats.shape, 1)
    levels = jnp.zeros(stats.shape, F32)
    for h in range(q.shape[1] // HD):
        cols = slice(h * HD, (h + 1) * HD)
        pieces = cached(kv_here, kv_there, cols) + [(k[:, cols], v[:, cols], same)]
        mixed, level = attend_pieces(q[:, cols], pieces)
        out[:, cols] = mixed
        levels = jnp.where(lane == h, level, levels)
    stats[...] = levels


def guest_kernel(group, q, kv_here, kv_there, out):
    local = out.shape[1] - LANES
    lane = lax.broadcasted_iota(jnp.int32, (out.shape[0], LANES), 1)
    tail = jnp.zeros(lane.shape, F32)
    for h in range(local // HD):
        cols = slice(h * HD, (h + 1) * HD)
        mixed, level = attend_pieces(q[:, cols], cached(kv_here, kv_there, cols))
        out[:, cols] = mixed.astype(BF)
        rest = jnp.broadcast_to(level, tail.shape)
        for i in range(3):
            piece = rest.astype(BF).astype(F32)
            tail = jnp.where(lane == 3 * h + i, piece, tail)
            rest = rest - piece
    out[:, local:] = tail.astype(BF)


def kv_specs(depth, some, part):
    return [
        pl.BlockSpec((1, depth, 2, some), lambda i, g: (0, 0, 0, g[0] * PARTS + part)),
        pl.BlockSpec((depth, 2, some), lambda i, g: (0, 0, part)),
    ]


def attend_own(group, part, q, kv, kv_there, k, v, seg_row, seg_col):
    rows, some = q.shape
    depth = kv.shape[1]
    block = pl.BlockSpec((rows, some), lambda i, g: (0, part))
    keys = 2 * depth + rows
    return pl.pallas_call(
        own_kernel,
        grid_spec=pltpu.PrefetchScalarGridSpec(
            num_scalar_prefetch=1,
            grid=(1,),
            in_specs=[whole((rows, some))]
            + kv_specs(depth, some, part)
            + [block, block, whole((rows, 1)), whole((1, rows))],
            out_specs=(whole((rows, some)), whole((rows, LANES))),
        ),
        out_shape=(
            jax.ShapeDtypeStruct((rows, some), F32),
            jax.ShapeDtypeStruct((rows, LANES), F32),
        ),
        compiler_params=params(20),
        cost_estimate=cost(4 * rows * keys * some, 4 * keys * some, rows * keys * some // HD),
        name="attend_own",
    )(group, q, kv, kv_there, k, v, seg_row, seg_col)


def attend_guest(group, part, q, kv, kv_there):
    rows, some = q.shape
    depth = kv.shape[1]
    keys = 2 * depth
    return pl.pallas_call(
        guest_kernel,
        grid_spec=pltpu.PrefetchScalarGridSpec(
            num_scalar_prefetch=1,
            grid=(1,),
            in_specs=[whole((rows, some))] + kv_specs(depth, some, part),
            out_specs=whole((rows, some + LANES)),
        ),
        out_shape=jax.ShapeDtypeStruct((rows, some + LANES), BF),
        compiler_params=params(20),
        cost_estimate=cost(4 * rows * keys * some, 4 * keys * some, rows * keys * some // HD),
        name="attend_guest",
    )(group, q, kv, kv_there)


def join_kernel(*refs):
    owns, levels, guests = (refs[i * PARTS : (i + 1) * PARTS] for i in range(3))
    w, keep, send = refs[3 * PARTS :]
    dev = keep.shape[0] // 2
    heads = []
    for own, stats, guest in zip(owns, levels, guests):
        some = own.shape[1]
        for h in range(some // HD):
            cols = slice(h * HD, (h + 1) * HD)
            first = stats[:, h : h + 1]
            start = some + 3 * h
            thirds = [guest[:, start + i : start + i + 1].astype(F32) for i in range(3)]
            second = functools.reduce(jnp.add, thirds)
            top = jnp.maximum(first, second)
            a, b = jnp.exp(first - top), jnp.exp(second - top)
            both = own[:, cols] * a + guest[:, cols].astype(F32) * b
            heads.append((both / (a + b)).astype(BF))
    mixed = jnp.concatenate(heads, axis=1)
    out = jnp.dot(mixed, w[...], preferred_element_type=F32)
    for i in range(2):
        keep[pl.ds(i * dev, dev), :] = out[2 * i * dev : (2 * i + 1) * dev]
        send[pl.ds(i * dev, dev), :] = out[(2 * i + 1) * dev : (2 * i + 2) * dev].astype(BF)


def join(owns, levels, guests, w):
    rows = owns[0].shape[0]
    local, width = w.shape
    return pl.pallas_call(
        join_kernel,
        out_shape=(
            jax.ShapeDtypeStruct((rows // 2, width), F32),
            jax.ShapeDtypeStruct((rows // 2, width), BF),
        ),
        compiler_params=params(20),
        cost_estimate=cost(2 * rows * local * width, 2 * local * width + 6 * rows * width // 2),
        name="join",
    )(*owns, *levels, *guests, w)


def entry_kernel(me, tokens, keep, arrived, gain, w_router, routes, resid, *messages):
    width = tokens.shape[1]
    experts = w_router.shape[1]
    values = tokens[...].astype(F32) + keep[...] + arrived[...].astype(F32)
    resid[...] = values
    mean_sq = jnp.mean(values * values, axis=-1, keepdims=True)
    normed = (values * lax.rsqrt(mean_sq + norm_eps) * gain[...]).astype(BF)
    logits = jnp.dot(normed, w_router[...], preferred_element_type=F32)
    lane = lax.broadcasted_iota(jnp.int32, logits.shape, 1)
    chosen = lane < 0
    for i in range(routes.shape[1]):
        chosen = chosen | (lane == routes[:, i : i + 1])
    logits = jnp.where(chosen, logits, -jnp.inf)
    expo = jnp.exp(logits - jnp.max(logits, axis=-1, keepdims=True))
    share = expo / jnp.sum(expo, axis=-1, keepdims=True)
    high = share.astype(BF)
    low = (share - high.astype(F32)).astype(BF)
    some = tokens.shape[0] // len(messages)
    for i, message in enumerate(messages):
        part = slice(i * some, (i + 1) * some)
        message[:, :width] = normed[part]
        message[:, width:] = jnp.zeros((some, LANES), BF)
        message[:, width : width + experts] = high[part]
        message[:, width + LANES // 2 : width + LANES // 2 + experts] = low[part]


def entry(me, tokens, keep, arrived, gain, w_router, routes, cuts):
    rows, width = tokens.shape
    some = rows // cuts
    experts, topk = w_router.shape[1], routes.shape[1]
    return pl.pallas_call(
        entry_kernel,
        grid_spec=pltpu.PrefetchScalarGridSpec(
            num_scalar_prefetch=1,
            grid=(1,),
            in_specs=[
                whole((rows, width)),
                whole((rows, width)),
                whole((rows, width)),
                whole((1, width)),
                whole((width, experts)),
                pl.BlockSpec((rows, topk), lambda i, m: (m[0], 0)),
            ],
            out_specs=(whole((rows, width)),) + (whole((some, width + LANES)),) * cuts,
        ),
        out_shape=(
            jax.ShapeDtypeStruct((rows, width), F32),
        )
        + (jax.ShapeDtypeStruct((some, width + LANES), BF),) * cuts,
        compiler_params=params(20),
        cost_estimate=cost(2 * rows * width * LANES, 12 * rows * width),
        name="entry",
    )(me, tokens, keep, arrived, gain, w_router, routes)


def expert_kernel(sizes, tile, group, *refs):
    count = len(sizes)
    pieces, (gate, up, down) = refs[:count], refs[count : count + 3]
    outs, (held, sems) = refs[count + 3 : -2], refs[-2:]
    experts, width = gate.shape[0], gate.shape[1]
    step = pl.program_id(0)

    @pl.when(step == 0)
    def _():
        start = 0
        for ref, size in zip(pieces, sizes):
            done = 0
            while done < size:
                take = min(size - done, tile - (start + done) % tile)
                pltpu.make_async_copy(
                    ref.at[pl.ds(done, take)],
                    held.at[pl.ds(start + done, take)],
                    sems.at[(start + done) // tile],
                ).start()
                done += take
            start += size

    here = pl.ds(pl.multiple_of(step * tile, tile), tile)
    pltpu.make_async_copy(held.at[here], held.at[here], sems.at[step]).wait()
    rows = held[here, :width]
    tail = held[here, width:].astype(F32)
    lane = lax.broadcasted_iota(jnp.int32, tail.shape, 1)
    result = None
    for e in range(experts):
        index = group[0] * experts + e
        hit = (lane == index) | (lane == index + LANES // 2)
        share = jnp.sum(jnp.where(hit, tail, 0.0), axis=1, keepdims=True)
        g = jnp.dot(rows, gate[e], preferred_element_type=F32)
        u = jnp.dot(rows, up[e], preferred_element_type=F32)
        act = (g * jax.nn.sigmoid(g) * u * share).astype(BF)
        one = jnp.dot(act, down[e], preferred_element_type=F32)
        result = one if result is None else result + one
    done = 0
    for out in outs:
        out[...] = result[done : done + out.shape[0]].astype(BF)
        done += out.shape[0]


def expert_part(group, pieces, weights, outs=1, most=512):
    gate = weights[0]
    sizes = [p.shape[0] for p in pieces]
    total = sum(sizes)
    tile = total if outs > 1 else next(t for t in range(most, 0, -64) if total % t == 0)
    wide, width = pieces[0].shape[1], gate.shape[1]
    some = tile // outs
    flops = 6 * total * gate.shape[0] * width * gate.shape[2]
    return pl.pallas_call(
        functools.partial(expert_kernel, sizes, tile),
        grid_spec=pltpu.PrefetchScalarGridSpec(
            num_scalar_prefetch=1,
            grid=(total // tile,),
            in_specs=[pl.BlockSpec(memory_space=pl.ANY)] * len(pieces)
            + [pl.BlockSpec(memory_space=pltpu.VMEM)] * 3,
            out_specs=(pl.BlockSpec((some, width), lambda i, g: (i, 0)),) * outs,
            scratch_shapes=[
                pltpu.VMEM((total, wide), BF),
                pltpu.SemaphoreType.DMA((total // tile,)),
            ],
        ),
        out_shape=(jax.ShapeDtypeStruct((total // outs, width), BF),) * outs,
        compiler_params=params(20 + (total >> 6)),
        cost_estimate=cost(flops, 4 * total * width + 6 * gate.size),
        name="experts",
    )(group, *pieces, *weights)


def add_bf(*values):
    return functools.reduce(jnp.add, [v.astype(F32) for v in values]).astype(BF)


def after(value, *others):
    return lax.optimization_barrier((value, *others))[0]


def join_rows(*values):
    return jnp.concatenate(values, axis=0)


def reduce_corner(kept, sent):
    total = add_bf(kept, move_c(sent))
    half = total.shape[0] // 2
    leaving = total[:half], total[half:]
    return (move_y(leaving[0]), move_x(leaving[1])), leaving


def reduce_rest(total, got):
    n = total.shape[0] // 3
    half = n // 2
    rows = n // (lax.axis_size("tok") // 2)
    here, by_y, by_x = (total[i * n : (i + 1) * n] for i in range(3))
    first = add_bf(by_x[:half], got[0])
    to_x = join_rows(first[rows:], by_x[half:])
    to_y = join_rows(by_y[rows:half], add_bf(by_y[half:], got[1]))
    rest = add_bf(here[rows:], move_x(to_x), move_y(to_y))
    return rest, (here[:rows], by_y[:rows], first[:rows]), (to_x, to_y)


def hold_kernel(count, *refs):
    sources, targets, sems = refs[:count], refs[count : 2 * count], refs[-1]
    copies = []
    for i in range(count):
        some = sources[i].shape[1] // sems.shape[2]
        for e in range(sources[i].shape[0]):
            for j in range(sems.shape[2]):
                rows = pl.ds(j * some, some)
                copies.append(
                    pltpu.make_async_copy(
                        sources[i].at[e, rows], targets[i].at[e, rows], sems.at[i, e, j]
                    )
                )
    for copy in copies:
        copy.start()
    for copy in copies:
        copy.wait()


def hold(*values):
    count = len(values)
    return pl.pallas_call(
        functools.partial(hold_kernel, count),
        out_shape=[jax.ShapeDtypeStruct(v.shape, v.dtype) for v in values],
        in_specs=[pl.BlockSpec(memory_space=pltpu.HBM)] * count,
        out_specs=[pl.BlockSpec(memory_space=pltpu.VMEM)] * count,
        scratch_shapes=[pltpu.SemaphoreType.DMA((count, values[0].shape[0], 2))],
        compiler_params=params(1),
        cost_estimate=cost(0, sum(4 * v.size for v in values)),
        name="hold",
    )(*in_hbm(*values))


def mixture(group, resid, messages, weights):
    rows = messages[0].shape[0]
    depth = lax.axis_size("tok") // 2
    n, half = depth * rows, depth * rows // 2
    first, second = messages

    first_z = [from_z(first, k) for k in range(1, depth)]
    second = after(second, *first_z)
    second_z = [from_z(second, k) for k in range(1, depth)]
    here_a = join_rows(first, *first_z)
    y_a, x_a = move_y(here_a), move_x(here_a)
    held = hold(*after(weights, y_a, x_a))
    corner_a = [move_y(x_a[:half]), move_x(y_a[half:])]
    main_a = [here_a, y_a, x_a]
    their_main_a, their_corner_a = ([move_c(v) for v in values] for values in (main_a, corner_a))
    (sent_a,) = expert_part(group, their_main_a, held)
    here_b = join_rows(second, *after(second_z, *corner_a))
    leaving_b = here_b
    y_b, x_b = move_y(leaving_b), move_x(leaving_b)
    (kept_a,) = expert_part(group, after(main_a, sent_a), held)
    sent_corner, kept_corner = expert_part(
        group, after(their_corner_a, kept_a) + corner_a, held, 2
    )
    got_a, _ = reduce_corner(after(kept_corner, y_b, x_b), sent_corner)

    corner_b = [move_y(x_b[:half]), move_x(y_b[half:])]
    main_b = [here_b, y_b, x_b]
    their_main_b = [move_c(v) for v in main_b]
    chip_a = add_bf(kept_a, move_c(sent_a))
    (sent_b,) = expert_part(group, after(their_main_b, sent_corner), held)
    (kept_b,) = expert_part(group, after(main_b, sent_b), held)
    corner_b = after(corner_b, kept_b)
    their_corner_b = [move_c(v) for v in corner_b]
    sent_corner, kept_corner = expert_part(group, their_corner_b + corner_b, held, 2)
    got_b, leaving_b = reduce_corner(kept_corner, sent_corner)
    chip_b = add_bf(kept_b, move_c(sent_b))
    rest_a, own_rows_a, _ = reduce_rest(chip_a, after(got_a, chip_b, *leaving_b))
    rest_b, own_rows_b, moving_b = reduce_rest(chip_b, got_b)

    def along_z(rest):
        parts = [rest[(k - 1) * rows : k * rows] for k in range(1, depth)]
        return [to_z(part, k) for k, part in zip(range(1, depth), parts)]

    landed_a = along_z(after(rest_a, *moving_b))
    landed_b = along_z(rest_b)
    here, to_y, to_x = (join_rows(u, v) for u, v in zip(own_rows_a, own_rows_b))
    to_y, to_x = after((to_y, to_x), rest_b)
    landed = [join_rows(u, v) for u, v in zip(landed_a, landed_b)]
    landed += [here, move_y(to_y), move_x(to_x)]
    return functools.reduce(jnp.add, [v.astype(F32) for v in landed], resid).astype(BF)


def request_layout(lengths_row, index):
    ends = jnp.cumsum(lengths_row)
    passed = (index[:, None] >= ends[None, :]).astype(jnp.int32)
    segment = jnp.sum(passed, axis=1)
    offset = index - jnp.sum(passed * lengths_row[None, :], axis=1)
    return segment, PREFIX + offset


def rotation(position):
    half = HD // 2
    freq = rope_base ** (-(jnp.arange(half).astype(F32) * 2.0) / HD)
    angle = position[:, None].astype(F32) * freq[None, :]
    cosine, sine = jnp.cos(angle), jnp.sin(angle)
    return jnp.concatenate([cosine, cosine], 1), jnp.concatenate([-sine, sine], 1)


def on_device(
    tokens, lengths, routes, prefix_kv, attn_gain, w_qkv, w_out, moe_gain, w_router, w_gate, w_up, w_down
):
    dev, width = tokens.shape
    local = w_qkv.shape[2]
    me = lax.axis_index("head")
    group = lax.axis_index("tok").astype(jnp.int32).reshape(1)

    by_c, by_y = move_c(tokens), move_y(tokens)
    mine = me.astype(jnp.int32).reshape(1)
    own_there, guest_there = stage(mine, prefix_kv, local)
    (w_held,) = hold(jnp.transpose(w_qkv, (1, 0, 2)))
    blocks = [tokens, by_c, by_y, move_c(after(by_y, w_held, guest_there))]

    own_there, guest_there = move_c(own_there), move_c(guest_there)

    index = ((me ^ jnp.arange(4))[:, None] * dev + jnp.arange(dev)[None, :]).reshape(-1)
    segment, position = request_layout(lengths[0], index)
    cosine, sine = rotation(position)

    *queries, k, v = project(blocks, attn_gain.reshape(1, -1), cosine, sine, w_held)
    guest_queries = [move_y(q) for q in queries]
    (cache,) = in_hbm(prefix_kv)
    seg_row, seg_col = segment.reshape(-1, 1), segment.reshape(1, -1)
    owns, guests, done = [], [], None
    owns.append(attend_own(mine, 0, queries[0], cache, own_there, k, v, seg_row, seg_col))
    for part in range(PARTS):
        q = after(guest_queries[part], owns[0][0])
        done = attend_guest(mine ^ 2, part, q, cache, guest_there)
        guests.append(move_y(done))
    for part in range(1, PARTS):
        q = after(queries[part], done, *guests[:-1])
        owns.append(attend_own(mine, part, q, cache, own_there, k, v, seg_row, seg_col))
    keep, send = join([o for o, _ in owns], [l for _, l in owns], guests, w_out)
    chip = keep + move_c(send).astype(F32)
    arrived = move_y(chip[dev:].astype(BF))
    resid, *messages = entry(
        mine, tokens, chip[:dev], arrived, moe_gain.reshape(1, -1), w_router, routes, CUTS
    )
    return mixture(group, resid, messages, (w_gate, w_up, w_down))


def solution(mesh):
    placed = (
        P(("tok", "head"), None),
        P("tok", None),
        P("tok", None),
        P("tok", "head", None, None),
        P(),
        P(None, None, "head"),
        P("head", None),
        P(),
        P(),
        P("tok", None, "head"),
        P("tok", None, "head"),
        P("tok", "head", None),
    )
    return jax.shard_map(
        on_device, mesh=mesh, in_specs=placed, out_specs=P(("tok", "head"), None), check_vma=False
    )
```
